512 devices in a mesh: dp: 4 (over x), tensor: 128 (over z, y, core).
Axes of the slice: x: 4, y: 8, z: 8, core: 2. Of those that a mesh axis runs over, the one named last changes fastest.
Arguments:
- hidden: bfloat16 [8192, 2048], P(('dp', 'tensor')), may hold values from -6 to 6
- norm_gain: float32 [2048], replicated, may hold values from 0.5 to 1.5
- head_weight: bfloat16 [2048, 102400], P('dp', 'tensor'), as said below
- token_ids: int32 [8192], P(('dp', 'tensor')), may hold values from 0 to 102399
- lengths: int32 [4, 4], P('dp'), may hold values from 1 to 512, 1024 in all within a row
Outputs:
- logprob: float32 [8192], P(('dp', 'tensor'))
- entropy: float32 [8192], P(('dp', 'tensor'))
The draws below stay inside these ranges and needn't reach their ends.
Inputs may be any that keep to these rules, and one draw needn't show every extreme that they name: Each index of dp has 4 lengths that sum to exactly 1024, and one of them equals 512. `head_weight`: head weights.
All inputs are finite; a program needn't handle non-finite values.
Results may differ from the reference program's by a relative error of at most 0.0045.
Values may be sent and summed in bfloat16 or wider, within the bound.
No kernel may reach another device: no remote copies, remote signals or barrier semaphores. Data moves between devices by JAX's collectives and lax.ppermute only.
A program may use at most 64 MiB of HBM per device.

```python
import math
import jax
import jax.numpy as jnp
import numpy as np
from jax import lax

D = 2048
V = 102400
SEQ_DP = 4
SLOT = 512
ROWS = 8192
N_DP = 4


def column_draw(key, index):
    return jax.random.normal(jax.random.fold_in(jax.random.fold_in(key, 11), index), (D,), jnp.float32)


def hot_pairs(key):
    order = jax.random.permutation(jax.random.fold_in(key, 13), V)
    pairs = order[:16].reshape(8, 2).astype(jnp.int32)
    target = 110.0 + 30.0 * jnp.arange(8, dtype=jnp.float32)
    scales = target / (1.5 * math.sqrt(D))
    return (pairs, target, scales)


def draw_head_weight(key, part):
    columns = jax.vmap(lambda index: column_draw(key, index))(jnp.arange(V))
    columns = jnp.clip(columns, -6.0, 6.0)
    spread = jnp.exp(jax.random.uniform(jax.random.fold_in(key, 12), (V,), jnp.float32, math.log(0.6), math.log(4.0)))
    pairs, target, scales = hot_pairs(key)
    columns = columns.at[pairs[:, 1]].set(columns[pairs[:, 0]])
    spread = spread.at[pairs[:, 0]].set(scales)
    spread = spread.at[pairs[:, 1]].set(scales * (1.0 - 2.0 / target))
    full = columns * (1.5 / math.sqrt(D) * spread)[:, None]
    return full.T.astype(jnp.bfloat16)


def draw_hidden(key, part):
    base = jnp.clip(jax.random.normal(jax.random.fold_in(key, 21), (ROWS, D), jnp.float32), -6.0, 6.0)
    pairs, target, scales = hot_pairs(key)
    aligned = jax.vmap(lambda index: jnp.clip(column_draw(key, index), -6.0, 6.0))(pairs[:, 0])
    aligned = aligned / jnp.max(jnp.abs(aligned), axis=1, keepdims=True) * 3.0
    places = jnp.arange(8, dtype=jnp.int32) * SLOT
    base = base.at[places].set(aligned)
    return base.astype(jnp.bfloat16)


def draw_token_ids(key, part):
    ids = jax.random.randint(jax.random.fold_in(key, 31), (ROWS,), 0, V).astype(jnp.int32)
    pairs, target, scales = hot_pairs(key)
    pick = jax.random.randint(jax.random.fold_in(key, 32), (8,), 0, 2).astype(jnp.int32)
    hot_ids = jnp.where(pick == 0, pairs[:, 0], pairs[:, 1])
    places = jnp.arange(8, dtype=jnp.int32) * SLOT
    return ids.at[places].set(hot_ids)


def profile(number_of, total, reach, skew):
    portions = [(1 << 20) // math.isqrt(grade ** skew) + 1 for grade in range(2, number_of + 1)]
    rest, counts = total - reach - (number_of - 1), [1] * (number_of - 1)
    while rest > 0:
        candidates = [i for i in range(number_of - 1) if counts[i] < reach]
        mass, remaining = sum([portions[i] for i in candidates]), rest
        for i in candidates:
            more = min(reach - counts[i], max(1, remaining * portions[i] // mass), rest)
            counts[i] = counts[i] + more
            rest = rest - more
    return np.array([reach] + counts)


def uneven_parts(key, number_of, total, bound, lean):
    if number_of == 2:
        one = jax.random.randint(key, (), max(1, total - bound), min(bound, total - 1) + 1)
        return jnp.stack([one, total - one])
    sizes = jnp.asarray(profile(number_of, total, bound, lean), jnp.int32)
    pairs = (number_of - 1) // 2
    giver, sink = sizes[1:1 + 2 * pairs:2], sizes[2:2 + 2 * pairs:2]
    slack = jnp.minimum(giver - 1, bound - sink)
    shifted = jax.random.randint(jax.random.fold_in(key, 1), (pairs,), 0, 1 << 20) % (slack + 1)
    sizes = sizes.at[1:1 + 2 * pairs:2].set(giver - shifted).at[2:2 + 2 * pairs:2].set(sink + shifted)
    return sizes[jax.random.permutation(jax.random.fold_in(key, 2), number_of)]


def setup_inputs(seed: int = 0) -> dict:
    splits = jax.random.split(jax.random.key(seed), 6)
    return {
        "hidden": draw_hidden(jax.random.fold_in(splits[5], 71), 0),
        "norm_gain": jnp.clip(1.0 + 0.1 * jax.random.normal(splits[1], (D,), jnp.float32), 0.5, 1.5),
        "head_weight": draw_head_weight(jax.random.fold_in(splits[5], 71), 0),
        "token_ids": draw_token_ids(jax.random.fold_in(splits[5], 71), 0),
        "lengths": jax.vmap(lambda own: uneven_parts(own, SEQ_DP, 2 * SLOT, SLOT, 2))(jax.random.split(splits[4], N_DP)).reshape((N_DP, SEQ_DP)).astype(jnp.int32),
    }


def reference(hidden, norm_gain, head_weight, token_ids, lengths):
    wide = hidden.astype(jnp.float32)
    meansq = lax.optimization_barrier(jnp.mean(wide * wide, axis=-1, keepdims=True))
    normed = (wide * lax.rsqrt(meansq + 1e-06) * norm_gain).astype(jnp.bfloat16)
    rows = jnp.arange(ROWS, dtype=jnp.int32)
    seqnum = rows // SLOT
    within = rows % SLOT
    scored = within < lengths.reshape(-1)[seqnum]
    block = 256
    count = ROWS // block

    def one_block(args):
        normed_blk, ids_blk = args
        logits = jnp.dot(normed_blk, head_weight, preferred_element_type=jnp.float32)
        top = lax.optimization_barrier(jnp.max(logits, axis=1))
        expo = jnp.exp(logits - top[:, None])
        total = lax.optimization_barrier(jnp.sum(expo, axis=1))
        moment = lax.optimization_barrier(jnp.sum(expo * logits, axis=1))
        chosen = jnp.take_along_axis(logits, ids_blk[:, None].astype(jnp.int32), axis=1)[:, 0]
        lse = top + jnp.log(total)
        return (chosen - lse, lse - moment / total)
    lprob, entro = lax.map(one_block, (normed.reshape(count, block, D), token_ids.reshape(count, block)))
    zero = jnp.zeros((ROWS,), jnp.float32)
    return (jnp.where(scored, lprob.reshape(-1), zero), jnp.where(scored, entro.reshape(-1), zero))
```

```python
import functools

import jax
import jax.numpy as jnp
from jax import lax
from jax.experimental import pallas as pl
from jax.experimental.pallas import tpu as pltpu
from jax.sharding import PartitionSpec as P

SEQ_DP = 4
SLOT = 512
BLOCK = 256
N_DP = 4


def head_kernel(len_ref, x_ref, ids_ref, w0, w1, w2, w3, out_ref, w_all, sem):
    step = pl.program_id(0)
    me = lax.axis_index("dp")
    vocab_dev, depth = w0.shape
    pieces = (w0, w1, w2, w3)

    @pl.when(step == 0)
    def _():
        copies = []
        for k in range(N_DP):
            src = lax.rem(me - k + N_DP, N_DP)
            copies.append(
                pltpu.make_async_copy(
                    pieces[k],
                    w_all.at[:, pl.ds(pl.multiple_of(src * depth, depth), depth)],
                    sem.at[k],
                )
            )
        for c in copies:
            c.start()
        for c in copies:
            c.wait()

    per_slot = SLOT // BLOCK
    live = len_ref[0, step // per_slot] > lax.rem(step, per_slot) * BLOCK

    @pl.when(live)
    def _():
        logits = lax.dot_general(
            w_all[...],
            x_ref[...],
            (((1,), (1,)), ((), ())),
            preferred_element_type=jnp.float32,
        )
        top = jnp.max(logits, axis=0, keepdims=True)
        expo = jnp.exp(logits - top)
        vocab = lax.axis_index("tensor") * vocab_dev + lax.broadcasted_iota(
            jnp.int32, logits.shape, 0
        )
        out_ref[0:1, :] = top
        out_ref[1:2, :] = jnp.sum(expo, axis=0, keepdims=True)
        out_ref[2:3, :] = jnp.sum(expo * logits, axis=0, keepdims=True)
        out_ref[3:4, :] = jnp.sum(
            jnp.where(vocab == ids_ref[...], logits, 0.0), axis=0, keepdims=True
        )

    @pl.when(jnp.logical_not(live))
    def _():
        out_ref[...] = jnp.zeros_like(out_ref)


def per_device(hidden, norm_gain, head_weight, token_ids, lengths):
    row_dev, width = hidden.shape
    vocab_dev = head_weight.shape[1]
    n_t = lax.axis_size("tensor")
    rows = row_dev * n_t
    tensor_idx = lax.axis_index("tensor")

    wide = hidden.astype(jnp.float32)
    meansq = jnp.mean(wide * wide, axis=-1, keepdims=True)
    normed = (wide * lax.rsqrt(meansq + 1e-06) * norm_gain).astype(jnp.bfloat16)
    pieces = [head_weight] + [
        lax.ppermute(head_weight, "dp", [(i, (i + k) % N_DP) for i in range(N_DP)])
        for k in range(1, N_DP)
    ]
    pieces = [p.T for p in pieces]
    everyone = lax.all_gather(normed, "tensor", axis=0, tiled=True)
    ids = lax.all_gather(token_ids, "tensor", axis=0, tiled=True)

    stats = pl.pallas_call(
        head_kernel,
        grid=(rows // BLOCK,),
        in_specs=[
            pl.BlockSpec(memory_space=pltpu.SMEM),
            pl.BlockSpec((BLOCK, width), lambda i: (i, 0)),
            pl.BlockSpec((1, BLOCK), lambda i: (0, i)),
        ]
        + [pl.BlockSpec(memory_space=pl.ANY)] * N_DP,
        out_specs=pl.BlockSpec((4, BLOCK), lambda i: (0, i)),
        out_shape=jax.ShapeDtypeStruct((4, rows), jnp.float32),
        scratch_shapes=[
            pltpu.VMEM((vocab_dev, width), jnp.bfloat16),
            pltpu.SemaphoreType.DMA((N_DP,)),
        ],
        compiler_params=pltpu.CompilerParams(vmem_limit_bytes=32 << 20),
        cost_estimate=pl.CostEstimate(
            flops=2 * rows * width * vocab_dev,
            bytes_accessed=2 * width * (rows + vocab_dev),
            transcendentals=rows * vocab_dev,
        ),
    )(lengths, everyone, ids[None, :], *pieces)

    sent = stats.reshape(4, n_t, row_dev).transpose(1, 0, 2).reshape(n_t, 4 * row_dev)
    back = lax.all_to_all(sent, "tensor", 0, 0).reshape(n_t, 4, row_dev)
    top, total, moment, chosen = (back[:, k] for k in range(4))
    top_own = jnp.max(top, axis=0)
    rescale = jnp.exp(top - top_own)
    total_own = jnp.sum(total * rescale, axis=0)
    moment_own = jnp.sum(moment * rescale, axis=0)
    chosen_own = jnp.sum(chosen, axis=0)

    own_rows = tensor_idx * row_dev + jnp.arange(row_dev, dtype=jnp.int32)
    onehot = (own_rows // SLOT)[:, None] == jnp.arange(SEQ_DP, dtype=jnp.int32)[None, :]
    length_of = jnp.sum(jnp.where(onehot, lengths[0][None, :], 0), axis=1)
    scored = own_rows % SLOT < length_of
    safe_total = jnp.where(scored, total_own, 1.0)
    lse = top_own + jnp.log(safe_total)
    logprob = jnp.where(scored, chosen_own - lse, 0.0)
    entropy = jnp.where(scored, lse - moment_own / safe_total, 0.0)
    return (logprob, entropy)


def solution(mesh):
    return jax.shard_map(
        per_device,
        mesh=mesh,
        in_specs=(
            P(("dp", "tensor"), None),
            P(),
            P("dp", "tensor"),
            P(("dp", "tensor")),
            P("dp", None),
        ),
        out_specs=(P(("dp", "tensor")), P(("dp", "tensor"))),
        check_vma=False,
    )
```

```python
import functools

import jax
import jax.numpy as jnp
from jax import lax
from jax.experimental import pallas as pl
from jax.experimental.pallas import tpu as pltpu
from jax.sharding import PartitionSpec as P

SEQ_DP = 4
SLOT = 512
N_DP = 4
N_Z, N_Y, N_CORE = 8, 8, 2
PER_CLASS = 2
CAP = 72
LANES = 128
DIGIT = 64
PITCH = SLOT // (N_Y * 2)
STATS = 4


def class_layout(len_ref, y_class, core):
    first = core * (N_Y * PER_CLASS) + y_class * PER_CLASS
    starts, counts, at = [], [], 0
    for s in range(SEQ_DP):
        n = jnp.clip(lax.div(len_ref[0, s] - first + (PITCH - 1), PITCH), 0, SLOT // PITCH)
        starts.append(at)
        counts.append(n * PER_CLASS)
        at = at + n * PER_CLASS
    return starts, counts


def my_place():
    t = lax.axis_index("tensor")
    return lax.rem(lax.div(t, N_CORE), N_Y), lax.rem(t, N_CORE)


def pack_kernel(len_ref, recv_ref, gain_ref, out_ref):
    width = gain_ref.shape[1]
    y, core = my_place()
    starts, counts = class_layout(len_ref, y, core)
    shape = (LANES, LANES)
    k = lax.broadcasted_iota(jnp.int32, shape, 0)
    i = lax.broadcasted_iota(jnp.int32, shape, 1)
    pick = jnp.zeros(shape, jnp.float32)
    for s in range(SEQ_DP):
        rel = k - starts[s]
        hit = (rel >= 0) & (rel < counts[s]) & (i == rel + s * (PER_CLASS * SLOT // PITCH))
        pick = jnp.where(hit, 1.0, pick)
    pick = pick.astype(jnp.bfloat16)
    rows = jnp.dot(pick[:CAP], recv_ref[:, :width], preferred_element_type=jnp.float32)
    meansq = jnp.mean(rows * rows, axis=-1, keepdims=True)
    normed = rows * lax.rsqrt(meansq + 1e-06) * gain_ref[...]
    digits = lax.dot_general(
        recv_ref[:, width:],
        pick,
        (((0,), (1,)), ((), ())),
        preferred_element_type=jnp.float32,
    ).astype(jnp.bfloat16)
    shape = (CAP, LANES)
    place = lax.broadcasted_iota(jnp.int32, shape, 0) - (CAP - 3)
    place = jnp.where(place == lax.broadcasted_iota(jnp.int32, shape, 1), 1.0, 0.0)
    tail = jnp.dot(place.astype(jnp.bfloat16), digits, preferred_element_type=jnp.float32)
    out_ref[...] = normed.astype(jnp.bfloat16)
    out_ref[:, :LANES] = (normed[:, :LANES] + tail).astype(jnp.bfloat16)


def head_kernel(offsets, last, len_ref, *refs):
    n = len(offsets)
    x_refs, w_refs = refs[:n], refs[n : n + 2 * N_DP]
    refs = refs[n + 2 * N_DP :]
    prev_ref = None
    if len(refs) == 4:
        prev_ref, refs = refs[0], refs[1:]
    out_ref, logit_ref, stat_ref = refs
    vocab_dev, depth = w_refs[0].shape
    y, core = my_place()
    me = lax.axis_index("dp")
    t = lax.axis_index("tensor")
    sibling = t + 1 - 2 * core
    wide = 2 * LANES

    x_all = jnp.concatenate([r[...] for r in x_refs], axis=0) if n > 1 else x_refs[0][...]
    ids = jnp.zeros((1, wide), jnp.float32)
    for j in range(n):
        d = x_refs[j][CAP - 8 :, :LANES].astype(jnp.float32)
        d = (d[5:6] * DIGIT + d[6:7]) * DIGIT + d[7:8]
        d = jnp.concatenate([d, jnp.zeros_like(d)], axis=1)
        ids = ids + (pltpu.roll(d, j * CAP, 1) if j else d)
    ids = ids[:, : n * CAP].astype(jnp.int32)

    for half, base in ((0, t), (1, sibling)):
        acc = None
        for k in range(N_DP):
            src = lax.rem(me - k + N_DP, N_DP)
            cols = pl.ds(pl.multiple_of(src * depth, depth), depth)
            x_k = jnp.concatenate([r[:, cols] for r in x_refs], axis=0)
            part = lax.dot_general(
                w_refs[half * N_DP + k][...],
                x_k,
                (((1,), (1,)), ((), ())),
                preferred_element_type=jnp.float32,
            )
            acc = part if acc is None else acc + part
        logit_ref[half * vocab_dev : (half + 1) * vocab_dev, :] = acc

    logits = logit_ref[...]
    row = lax.broadcasted_iota(jnp.int32, logits.shape, 0)
    vocab = row + jnp.where(row < vocab_dev, t * vocab_dev, (sibling - 1) * vocab_dev)
    top = jnp.max(logits, axis=0, keepdims=True)
    expo = jnp.exp(logits - top)
    stat_ref[...] = jnp.zeros_like(stat_ref)
    stat_ref[0:1, : n * CAP] = top
    stat_ref[1:2, : n * CAP] = jnp.sum(expo, axis=0, keepdims=True)
    stat_ref[2:3, : n * CAP] = jnp.sum(expo * logits, axis=0, keepdims=True)
    stat_ref[3:4, : n * CAP] = jnp.sum(
        jnp.where(vocab == ids, logits, 0.0), axis=0, keepdims=True
    )

    if prev_ref is not None:
        out_ref[...] = prev_ref[...]
    lane = lax.broadcasted_iota(jnp.int32, (8, LANES), 1)
    per_slot = PER_CLASS * SLOT // PITCH
    stats = stat_ref[...]
    for j, offset in enumerate(offsets):
        y_class = lax.rem(y + offset + N_Y, N_Y)
        starts, _ = class_layout(len_ref, y_class, core)
        spread = jnp.zeros((8, LANES), jnp.float32)
        for s in range(SEQ_DP):
            shift = lax.rem(s * per_slot - j * CAP - starts[s] + 2 * wide, wide)
            moved = pltpu.roll(stats, shift, 1)[:, :LANES]
            spread = jnp.where(lane // per_slot == s, moved, spread)
        out_ref[pl.ds(y_class, 1)] = spread[None]


def run_head(offsets, lengths, shards, weights, prev):
    n = len(offsets)
    vocab_dev, depth = weights[0].shape
    vmem = pl.BlockSpec(memory_space=pltpu.VMEM)
    args = [lengths, *shards, *weights] + ([] if prev is None else [prev])
    return pl.pallas_call(
        functools.partial(head_kernel, offsets, False),
        in_specs=[pl.BlockSpec(memory_space=pltpu.SMEM)] + [vmem] * (len(args) - 1),
        out_specs=vmem,
        out_shape=jax.ShapeDtypeStruct((N_Y, 8, LANES), jnp.float32),
        scratch_shapes=[
            pltpu.VMEM((2 * vocab_dev, n * CAP), jnp.float32),
            pltpu.VMEM((8, 2 * LANES), jnp.float32),
        ],
        compiler_params=pltpu.CompilerParams(vmem_limit_bytes=40 << 20),
        cost_estimate=pl.CostEstimate(
            flops=2 * n * CAP * depth * N_DP * 2 * vocab_dev,
            bytes_accessed=2 * depth * N_DP * (n * CAP + 2 * vocab_dev),
            transcendentals=n * CAP * 2 * vocab_dev,
        ),
    )(*args)


def per_device(hidden, norm_gain, head_weight, token_ids, lengths):
    row_dev, width = hidden.shape
    n_t = N_Z * N_Y * N_CORE
    n_chip = N_Z * N_Y
    tensor_idx = lax.axis_index("tensor")
    same_core = [[N_CORE * k + c for k in range(n_chip)] for c in range(N_CORE)]
    other_core = [(i, i ^ 1) for i in range(n_t)]

    def along_y(by):
        step = []
        for i in range(n_t):
            y = (i // N_CORE) % N_Y
            step.append((i, i + ((y + by) % N_Y - y) * N_CORE))
        return step

    pieces = [head_weight] + [
        lax.ppermute(head_weight, "dp", [(i, (i + k) % N_DP) for i in range(N_DP)])
        for k in (1, 2, 3)
    ]

    digits = jnp.stack(
        [token_ids // (DIGIT * DIGIT), token_ids // DIGIT % DIGIT, token_ids % DIGIT], axis=1
    ).astype(jnp.bfloat16)
    digits = jnp.pad(digits, ((0, 0), (0, LANES - 3)))
    sent = jnp.concatenate([hidden, digits], axis=1).reshape(N_Y, PER_CLASS, width + LANES)
    sent = jnp.broadcast_to(sent[None], (N_Z,) + sent.shape).reshape(
        n_chip, PER_CLASS, width + LANES
    )
    recv = lax.all_to_all(sent, "tensor", 0, 0, axis_index_groups=same_core)
    recv = recv.reshape(n_chip * PER_CLASS, width + LANES)

    vmem = pl.BlockSpec(memory_space=pltpu.VMEM)
    own = pl.pallas_call(
        pack_kernel,
        in_specs=[pl.BlockSpec(memory_space=pltpu.SMEM), vmem, vmem],
        out_specs=vmem,
        out_shape=jax.ShapeDtypeStruct((CAP, width), jnp.bfloat16),
        cost_estimate=pl.CostEstimate(
            flops=2 * CAP * LANES * width, bytes_accessed=2 * (CAP + LANES) * width, transcendentals=0
        ),
    )(lengths, recv, norm_gain[None, :])

    up = [own]
    down = [own]
    for _ in range(N_Y // 2 - 1):
        pair = (
            lax.ppermute(up[-1], "tensor", along_y(1)),
            lax.ppermute(down[-1], "tensor", along_y(-1)),
        )
        pair = lax.optimization_barrier(pair)
        up.append(pair[0])
        down.append(pair[1])
    up.append(lax.ppermute(up[-1], "tensor", along_y(1)))

    late = lax.optimization_barrier((*pieces[1:], up[2], down[2]))
    weights = [p.T for p in pieces]
    weights += [
        lax.ppermute(p, "tensor", other_core).T for p in (head_weight, *late[: N_DP - 1])
    ]
    stats = run_head((0, -1, 1), lengths, [own, up[1], down[1]], weights, None)
    stats = run_head((-2, 2), lengths, [up[2], down[2]], weights, stats)
    stats = run_head((-3, 3, -4), lengths, [up[3], down[3], up[4]], weights, stats)

    sent = stats[:, :STATS].reshape(N_Y, STATS, n_chip, PER_CLASS)
    sent = sent.transpose(2, 1, 0, 3).reshape(n_chip, STATS * row_dev)
    back = lax.all_to_all(sent, "tensor", 0, 0, axis_index_groups=same_core)
    back = back.reshape(n_chip, STATS, row_dev)
    top, total, moment, chosen = (back[:, k] for k in range(STATS))
    top_own = jnp.max(top, axis=0)
    rescale = jnp.exp(top - top_own)
    total_own = jnp.sum(total * rescale, axis=0)
    moment_own = jnp.sum(moment * rescale, axis=0)
    chosen_own = jnp.sum(chosen, axis=0)

    own_rows = tensor_idx * row_dev + jnp.arange(row_dev, dtype=jnp.int32)
    onehot = (own_rows // SLOT)[:, None] == jnp.arange(SEQ_DP, dtype=jnp.int32)[None, :]
    length_of = jnp.sum(jnp.where(onehot, lengths[0][None, :], 0), axis=1)
    scored = own_rows % SLOT < length_of
    safe_total = jnp.where(scored, total_own, 1.0)
    lse = top_own + jnp.log(safe_total)
    logprob = jnp.where(scored, chosen_own - lse, 0.0)
    entropy = jnp.where(scored, lse - moment_own / safe_total, 0.0)
    return (logprob, entropy)


def solution(mesh):
    return jax.shard_map(
        per_device,
        mesh=mesh,
        in_specs=(
            P(("dp", "tensor"), None),
            P(),
            P("dp", "tensor"),
            P(("dp", "tensor")),
            P("dp", None),
        ),
        out_specs=(P(("dp", "tensor")), P(("dp", "tensor"))),
        check_vma=False,
    )
```

```python
import functools

import jax
import jax.numpy as jnp
from jax import lax
from jax.experimental import pallas as pl
from jax.experimental.pallas import tpu as pltpu
from jax.sharding import PartitionSpec as P

SEQ_DP = 4
SLOT = 512
N_DP = 4
N_Z, N_Y, N_CORE = 8, 8, 2
PER_CLASS = 2
CAP = 72
LANES = 128
DIGIT = 64
TILE = 400
PITCH = SLOT // (N_Y * 2)
STATS = 4


def class_layout(len_ref, y_class, core):
    first = core * (N_Y * PER_CLASS) + y_class * PER_CLASS
    starts, counts, at = [], [], 0
    for s in range(SEQ_DP):
        n = jnp.clip(lax.div(len_ref[0, s] - first + (PITCH - 1), PITCH), 0, SLOT // PITCH)
        starts.append(at)
        counts.append(n * PER_CLASS)
        at = at + n * PER_CLASS
    return starts, counts


def my_place():
    t = lax.axis_index("tensor")
    return lax.rem(lax.div(t, N_CORE), N_Y), lax.rem(t, N_CORE)


def pack_kernel(len_ref, recv_ref, gain_ref, out_ref):
    width = gain_ref.shape[1]
    y, core = my_place()
    starts, counts = class_layout(len_ref, y, core)
    shape = (LANES, LANES)
    k = lax.broadcasted_iota(jnp.int32, shape, 0)
    i = lax.broadcasted_iota(jnp.int32, shape, 1)
    pick = jnp.zeros(shape, jnp.float32)
    for s in range(SEQ_DP):
        rel = k - starts[s]
        hit = (rel >= 0) & (rel < counts[s]) & (i == rel + s * (PER_CLASS * SLOT // PITCH))
        pick = jnp.where(hit, 1.0, pick)
    pick = pick.astype(jnp.bfloat16)
    rows = jnp.dot(pick[:CAP], recv_ref[:, :width], preferred_element_type=jnp.float32)
    meansq = jnp.mean(rows * rows, axis=-1, keepdims=True)
    normed = rows * lax.rsqrt(meansq + 1e-06) * gain_ref[...]
    digits = lax.dot_general(
        recv_ref[:, width:],
        pick,
        (((0,), (1,)), ((), ())),
        preferred_element_type=jnp.float32,
    ).astype(jnp.bfloat16)
    shape = (CAP, LANES)
    place = lax.broadcasted_iota(jnp.int32, shape, 0) - (CAP - 3)
    place = jnp.where(place == lax.broadcasted_iota(jnp.int32, shape, 1), 1.0, 0.0)
    tail = jnp.dot(place.astype(jnp.bfloat16), digits, preferred_element_type=jnp.float32)
    out_ref[...] = normed.astype(jnp.bfloat16)
    out_ref[:, :LANES] = (normed[:, :LANES] + tail).astype(jnp.bfloat16)


def stack_kernel(w0, w1, w2, w3, out_ref, sem):
    me = lax.axis_index("dp")
    depth = w0.shape[1]
    copies = []
    for k, piece in enumerate((w0, w1, w2, w3)):
        src = lax.rem(me - k + N_DP, N_DP)
        cols = pl.ds(pl.multiple_of(src * depth, depth), depth)
        copies.append(pltpu.make_async_copy(piece, out_ref.at[:, cols], sem.at[k]))
    for c in copies:
        c.start()
    for c in copies:
        c.wait()


def head_kernel(offsets, len_ref, *refs):
    n = len(offsets)
    x_refs, w_refs, refs = refs[:n], refs[n : n + 2], refs[n + 2 :]
    prev_ref = None
    if len(refs) == 3:
        prev_ref, refs = refs[0], refs[1:]
    out_ref, stat_ref = refs
    vocab_dev = w_refs[0].shape[0]
    y, core = my_place()
    t = lax.axis_index("tensor")
    sibling = t + 1 - 2 * core
    wide = 2 * LANES

    x_all = jnp.concatenate([r[...] for r in x_refs], axis=0)
    ids = jnp.zeros((1, wide), jnp.float32)
    for j in range(n):
        d = x_refs[j][CAP - 8 :, :LANES].astype(jnp.float32)
        d = (d[5:6] * DIGIT + d[6:7]) * DIGIT + d[7:8]
        d = jnp.concatenate([d, jnp.zeros_like(d)], axis=1)
        ids = ids + (pltpu.roll(d, j * CAP, 1) if j else d)
    ids = ids[:, : n * CAP].astype(jnp.int32)

    parts = []
    for w_ref, owner in zip(w_refs, (t, sibling)):
        for at in range(0, vocab_dev, TILE):
            logits = lax.dot_general(
                w_ref[at : at + TILE, :],
                x_all,
                (((1,), (1,)), ((), ())),
                preferred_element_type=jnp.float32,
            )
            row = lax.broadcasted_iota(jnp.int32, logits.shape, 0)
            top = jnp.max(logits, axis=0, keepdims=True)
            expo = jnp.exp(logits - top)
            total = jnp.sum(expo, axis=0, keepdims=True)
            moment = jnp.sum(expo * logits, axis=0, keepdims=True)
            hit = row == ids - (owner * vocab_dev + at)
            chosen = jnp.sum(jnp.where(hit, logits, 0.0), axis=0, keepdims=True)
            parts.append((top, total, moment, chosen))
    top = functools.reduce(jnp.maximum, [p[0] for p in parts])
    scale = [jnp.exp(p[0] - top) for p in parts]
    stat_ref[...] = jnp.zeros_like(stat_ref)
    stat_ref[0:1, : n * CAP] = top
    stat_ref[1:2, : n * CAP] = sum(p[1] * f for p, f in zip(parts, scale))
    stat_ref[2:3, : n * CAP] = sum(p[2] * f for p, f in zip(parts, scale))
    stat_ref[3:4, : n * CAP] = sum(p[3] for p in parts)

    if prev_ref is not None:
        out_ref[...] = prev_ref[...]
    lane = lax.broadcasted_iota(jnp.int32, (8, LANES), 1)
    per_slot = PER_CLASS * SLOT // PITCH
    stats = stat_ref[...]
    for j, offset in enumerate(offsets):
        y_class = lax.rem(y + offset + N_Y, N_Y)
        starts, _ = class_layout(len_ref, y_class, core)
        spread = jnp.zeros((8, LANES), jnp.float32)
        for s in range(SEQ_DP):
            shift = lax.rem(s * per_slot - j * CAP - starts[s] + 2 * wide, wide)
            moved = pltpu.roll(stats, shift, 1)[:, :LANES]
            spread = jnp.where(lane // per_slot == s, moved, spread)
        out_ref[pl.ds(y_class, 1)] = spread[None]


def run_head(offsets, lengths, shards, weights, prev):
    n = len(offsets)
    vocab_dev, width = weights[0].shape
    vmem = pl.BlockSpec(memory_space=pltpu.VMEM)
    args = [lengths, *shards, *weights] + ([] if prev is None else [prev])
    return pl.pallas_call(
        functools.partial(head_kernel, offsets),
        in_specs=[pl.BlockSpec(memory_space=pltpu.SMEM)] + [vmem] * (len(args) - 1),
        out_specs=vmem,
        out_shape=jax.ShapeDtypeStruct((N_Y, 8, LANES), jnp.float32),
        scratch_shapes=[pltpu.VMEM((8, 2 * LANES), jnp.float32)],
        compiler_params=pltpu.CompilerParams(vmem_limit_bytes=40 << 20),
        cost_estimate=pl.CostEstimate(
            flops=2 * n * CAP * width * 2 * vocab_dev,
            bytes_accessed=2 * width * (n * CAP + 2 * vocab_dev),
            transcendentals=n * CAP * 2 * vocab_dev,
        ),
    )(*args)


def per_device(hidden, norm_gain, head_weight, token_ids, lengths):
    row_dev, width = hidden.shape
    n_t = N_Z * N_Y * N_CORE
    n_chip = N_Z * N_Y
    tensor_idx = lax.axis_index("tensor")
    same_core = [[N_CORE * k + c for k in range(n_chip)] for c in range(N_CORE)]
    other_core = [(i, i ^ 1) for i in range(n_t)]

    def along_y(by):
        step = []
        for i in range(n_t):
            y = (i // N_CORE) % N_Y
            step.append((i, i + ((y + by) % N_Y - y) * N_CORE))
        return step

    pieces = [head_weight] + [
        lax.ppermute(head_weight, "dp", [(i, (i + k) % N_DP) for i in range(N_DP)])
        for k in (1, 2, 3)
    ]

    digits = jnp.stack(
        [token_ids // (DIGIT * DIGIT), token_ids // DIGIT % DIGIT, token_ids % DIGIT], axis=1
    ).astype(jnp.bfloat16)
    digits = jnp.pad(digits, ((0, 0), (0, LANES - 3)))
    sent = jnp.concatenate([hidden, digits], axis=1).reshape(N_Y, PER_CLASS, width + LANES)
    sent = jnp.broadcast_to(sent[None], (N_Z,) + sent.shape).reshape(
        n_chip, PER_CLASS, width + LANES
    )
    recv = lax.all_to_all(sent, "tensor", 0, 0, axis_index_groups=same_core)
    recv = recv.reshape(n_chip * PER_CLASS, width + LANES)

    vmem = pl.BlockSpec(memory_space=pltpu.VMEM)
    own = pl.pallas_call(
        pack_kernel,
        in_specs=[pl.BlockSpec(memory_space=pltpu.SMEM), vmem, vmem],
        out_specs=vmem,
        out_shape=jax.ShapeDtypeStruct((CAP, width), jnp.bfloat16),
        cost_estimate=pl.CostEstimate(
            flops=2 * CAP * LANES * width, bytes_accessed=2 * (CAP + LANES) * width, transcendentals=0
        ),
    )(lengths, recv, norm_gain[None, :])

    up = [own]
    down = [own]
    for _ in range(N_Y // 2 - 1):
        pair = (
            lax.ppermute(up[-1], "tensor", along_y(1)),
            lax.ppermute(down[-1], "tensor", along_y(-1)),
        )
        pair = lax.optimization_barrier(pair)
        up.append(pair[0])
        down.append(pair[1])
    up.append(lax.ppermute(up[-1], "tensor", along_y(1)))

    late = lax.optimization_barrier((*pieces, up[2], down[2]))
    anywhere = pl.BlockSpec(memory_space=pl.ANY)
    vocab_dev = head_weight.shape[1]
    weight = pl.pallas_call(
        stack_kernel,
        in_specs=[anywhere] * N_DP,
        out_specs=anywhere,
        out_shape=jax.ShapeDtypeStruct((vocab_dev, width), jnp.bfloat16),
        scratch_shapes=[pltpu.SemaphoreType.DMA((N_DP,))],
        cost_estimate=pl.CostEstimate(
            flops=0, bytes_accessed=4 * vocab_dev * width, transcendentals=0
        ),
    )(*[p.T for p in late[:N_DP]])
    weights = [weight, lax.ppermute(weight, "tensor", other_core)]
    stats = run_head((0, -1, 1), lengths, [own, up[1], down[1]], weights, None)
    stats = run_head((-2, 2), lengths, [up[2], down[2]], weights, stats)
    stats = run_head((-3, 3, -4), lengths, [up[3], down[3], up[4]], weights, stats)

    sent = stats[:, :STATS].reshape(N_Y, STATS, n_chip, PER_CLASS)
    sent = sent.transpose(2, 1, 0, 3).reshape(n_chip, STATS * row_dev)
    back = lax.all_to_all(sent, "tensor", 0, 0, axis_index_groups=same_core)
    back = back.reshape(n_chip, STATS, row_dev)
    top, total, moment, chosen = (back[:, k] for k in range(STATS))
    top_own = jnp.max(top, axis=0)
    rescale = jnp.exp(top - top_own)
    total_own = jnp.sum(total * rescale, axis=0)
    moment_own = jnp.sum(moment * rescale, axis=0)
    chosen_own = jnp.sum(chosen, axis=0)

    own_rows = tensor_idx * row_dev + jnp.arange(row_dev, dtype=jnp.int32)
    onehot = (own_rows // SLOT)[:, None] == jnp.arange(SEQ_DP, dtype=jnp.int32)[None, :]
    length_of = jnp.sum(jnp.where(onehot, lengths[0][None, :], 0), axis=1)
    scored = own_rows % SLOT < length_of
    safe_total = jnp.where(scored, total_own, 1.0)
    lse = top_own + jnp.log(safe_total)
    logprob = jnp.where(scored, chosen_own - lse, 0.0)
    entropy = jnp.where(scored, lse - moment_own / safe_total, 0.0)
    return (logprob, entropy)


def solution(mesh):
    return jax.shard_map(
        per_device,
        mesh=mesh,
        in_specs=(
            P(("dp", "tensor"), None),
            P(),
            P("dp", "tensor"),
            P(("dp", "tensor")),
            P("dp", None),
        ),
        out_specs=(P(("dp", "tensor")), P(("dp", "tensor"))),
        check_vma=False,
    )
```

```python
import functools

import jax
import jax.numpy as jnp
from jax import lax
from jax.experimental import pallas as pl
from jax.experimental.pallas import tpu as pltpu
from jax.sharding import PartitionSpec as P

SEQ_DP = 4
SLOT = 512
N_DP = 4
N_Z, N_Y, N_CORE = 8, 8, 2
PER_CLASS = 2
CAP = 72
LANES = 128
DIGIT = 64
TILE = 400
PITCH = SLOT // (N_Y * 2)
STATS = 4


def class_layout(len_ref, place, core):
    first = core * (N_Y * PER_CLASS) + place * PER_CLASS
    starts, counts, at = [], [], 0
    for s in range(SEQ_DP):
        n = jnp.clip(lax.div(len_ref[0, s] - first + (PITCH - 1), PITCH), 0, SLOT // PITCH)
        starts.append(at)
        counts.append(n * PER_CLASS)
        at = at + n * PER_CLASS
    return starts, counts


def my_place():
    t = lax.axis_index("tensor")
    core = lax.rem(t, N_CORE)
    y = lax.rem(lax.div(t, N_CORE), N_Y)
    z = lax.div(t, N_CORE * N_Y)
    return jnp.where(core == 0, y, z), core


def pack_kernel(len_ref, recv_ref, gain_ref, out_ref):
    width = gain_ref.shape[1]
    mine, core = my_place()
    starts, counts = class_layout(len_ref, mine, core)
    shape = (LANES, LANES)
    k = lax.broadcasted_iota(jnp.int32, shape, 0)
    i = lax.broadcasted_iota(jnp.int32, shape, 1)
    pick = jnp.zeros(shape, jnp.float32)
    for s in range(SEQ_DP):
        rel = k - starts[s]
        hit = (rel >= 0) & (rel < counts[s]) & (i == rel + s * (PER_CLASS * SLOT // PITCH))
        pick = jnp.where(hit, 1.0, pick)
    pick = pick.astype(jnp.bfloat16)
    rows = jnp.dot(pick[:CAP], recv_ref[:, :width], preferred_element_type=jnp.float32)
    meansq = jnp.mean(rows * rows, axis=-1, keepdims=True)
    normed = rows * lax.rsqrt(meansq + 1e-06) * gain_ref[...]
    digits = lax.dot_general(
        recv_ref[:, width:],
        pick,
        (((0,), (1,)), ((), ())),
        preferred_element_type=jnp.float32,
    ).astype(jnp.bfloat16)
    shape = (CAP, LANES)
    place = lax.broadcasted_iota(jnp.int32, shape, 0) - (CAP - 3)
    place = jnp.where(place == lax.broadcasted_iota(jnp.int32, shape, 1), 1.0, 0.0)
    tail = jnp.dot(place.astype(jnp.bfloat16), digits, preferred_element_type=jnp.float32)
    out_ref[...] = normed.astype(jnp.bfloat16)
    out_ref[:, :LANES] = (normed[:, :LANES] + tail).astype(jnp.bfloat16)


def stack_kernel(w0, w1, w2, w3, up_ref, down_ref, out_ref, sem):
    del up_ref, down_ref
    me = lax.axis_index("dp")
    depth = w0.shape[1]
    copies = []
    for k, piece in enumerate((w0, w1, w2, w3)):
        src = lax.rem(me - k + N_DP, N_DP)
        cols = pl.ds(pl.multiple_of(src * depth, depth), depth)
        copies.append(pltpu.make_async_copy(piece, out_ref.at[:, cols], sem.at[k]))
    for c in copies:
        c.start()
    for c in copies:
        c.wait()


def head_kernel(offsets, len_ref, *refs):
    n = len(offsets)
    x_refs, w_refs, refs = refs[:n], refs[n : n + 2], refs[n + 2 :]
    prev_ref = None
    if len(refs) == 6:
        prev_ref, refs = refs[0], refs[1:]
    out_ref, stat_ref, x_ref, w_ref, sem = refs
    vocab_dev = w_refs[0].shape[0]
    mine, core = my_place()
    t = lax.axis_index("tensor")
    sibling = t + 1 - 2 * core
    wide = 2 * LANES

    copies = [pltpu.make_async_copy(r, x_ref.at[j], sem.at[j]) for j, r in enumerate(x_refs)]
    tiles = []
    for half, ref in enumerate(w_refs):
        for at in range(0, vocab_dev, TILE):
            i = len(tiles)
            copy = pltpu.make_async_copy(ref.at[at : at + TILE, :], w_ref.at[i], sem.at[n + i])
            tiles.append((copy, half, at))
    for c in copies + [tile[0] for tile in tiles]:
        c.start()
    for c in copies:
        c.wait()
    x_all = jnp.concatenate([x_ref[j] for j in range(n)], axis=0)
    ids = jnp.zeros((1, wide), jnp.float32)
    for j in range(n):
        d = x_ref[j, CAP - 8 :, :LANES].astype(jnp.float32)
        d = (d[5:6] * DIGIT + d[6:7]) * DIGIT + d[7:8]
        d = jnp.concatenate([d, jnp.zeros_like(d)], axis=1)
        ids = ids + (pltpu.roll(d, j * CAP, 1) if j else d)
    ids = ids[:, : n * CAP].astype(jnp.int32)

    parts = []
    for i, (copy, half, at) in enumerate(tiles):
        owner = sibling if half else t
        copy.wait()
        logits = lax.dot_general(
            w_ref[i],
            x_all,
            (((1,), (1,)), ((), ())),
            preferred_element_type=jnp.float32,
        )
        row = lax.broadcasted_iota(jnp.int32, logits.shape, 0)
        top = jnp.max(logits, axis=0, keepdims=True)
        expo = jnp.exp(logits - top)
        total = jnp.sum(expo, axis=0, keepdims=True)
        moment = jnp.sum(expo * logits, axis=0, keepdims=True)
        hit = row == ids - (owner * vocab_dev + at)
        chosen = jnp.sum(jnp.where(hit, logits, 0.0), axis=0, keepdims=True)
        parts.append((top, total, moment, chosen))
    top = functools.reduce(jnp.maximum, [p[0] for p in parts])
    scale = [jnp.exp(p[0] - top) for p in parts]
    stat_ref[...] = jnp.zeros_like(stat_ref)
    stat_ref[0:1, : n * CAP] = top
    stat_ref[1:2, : n * CAP] = sum(p[1] * f for p, f in zip(parts, scale))
    stat_ref[2:3, : n * CAP] = sum(p[2] * f for p, f in zip(parts, scale))
    stat_ref[3:4, : n * CAP] = sum(p[3] for p in parts)

    if prev_ref is not None:
        out_ref[...] = prev_ref[...]
    lane = lax.broadcasted_iota(jnp.int32, (8, LANES), 1)
    per_slot = PER_CLASS * SLOT // PITCH
    stats = stat_ref[...]
    for j, offset in enumerate(offsets):
        place = lax.rem(mine + offset + N_Y, N_Y)
        starts, _ = class_layout(len_ref, place, core)
        spread = jnp.zeros((8, LANES), jnp.float32)
        for s in range(SEQ_DP):
            shift = lax.rem(s * per_slot - j * CAP - starts[s] + 2 * wide, wide)
            moved = pltpu.roll(stats, shift, 1)[:, :LANES]
            spread = jnp.where(lane // per_slot == s, moved, spread)
        out_ref[pl.ds(place, 1)] = spread[None]


def run_head(offsets, lengths, shards, weights, prev):
    n = len(offsets)
    vocab_dev, width = weights[0].shape
    vmem = pl.BlockSpec(memory_space=pltpu.VMEM)
    anywhere = pl.BlockSpec(memory_space=pl.ANY)
    args = [lengths, *shards, *weights] + ([] if prev is None else [prev])
    return pl.pallas_call(
        functools.partial(head_kernel, offsets),
        in_specs=[pl.BlockSpec(memory_space=pltpu.SMEM)]
        + [anywhere] * (n + 2)
        + [vmem] * (len(args) - 3 - n),
        out_specs=vmem,
        out_shape=jax.ShapeDtypeStruct((N_Y, 8, LANES), jnp.float32),
        scratch_shapes=[
            pltpu.VMEM((8, 2 * LANES), jnp.float32),
            pltpu.VMEM((n, CAP, width), jnp.bfloat16),
            pltpu.VMEM((2 * vocab_dev // TILE, TILE, width), jnp.bfloat16),
            pltpu.SemaphoreType.DMA((n + 2 * vocab_dev // TILE,)),
        ],
        cost_estimate=pl.CostEstimate(
            flops=2 * n * CAP * width * 2 * vocab_dev,
            bytes_accessed=2 * width * (n * CAP + 2 * vocab_dev),
            transcendentals=n * CAP * 2 * vocab_dev,
        ),
    )(*args)


def per_device(hidden, norm_gain, head_weight, token_ids, lengths):
    row_dev, width = hidden.shape
    n_t = N_Z * N_Y * N_CORE
    n_chip = N_Z * N_Y
    tensor_idx = lax.axis_index("tensor")
    same_core = [[N_CORE * k + c for k in range(n_chip)] for c in range(N_CORE)]
    other_core = [(i, i ^ 1) for i in range(n_t)]

    def along(by):
        step = []
        for i in range(n_t):
            z, y, core = i // (N_Y * N_CORE), i // N_CORE % N_Y, i % N_CORE
            if core == 0:
                y = (y + by) % N_Y
            else:
                z = (z + by) % N_Z
            step.append((i, (z * N_Y + y) * N_CORE + core))
        return step

    pieces = [head_weight] + [
        lax.ppermute(head_weight, "dp", [(i, (i + k) % N_DP) for i in range(N_DP)])
        for k in (1, 2, 3)
    ]

    digits = jnp.stack(
        [token_ids // (DIGIT * DIGIT), token_ids // DIGIT % DIGIT, token_ids % DIGIT], axis=1
    ).astype(jnp.bfloat16)
    digits = jnp.pad(digits, ((0, 0), (0, LANES - 3)))
    sent = jnp.concatenate([hidden, digits], axis=1).reshape(N_Y, PER_CLASS, width + LANES)
    square = (N_Z, N_Y) + sent.shape[1:]
    sent = jnp.where(
        tensor_idx % N_CORE == 0,
        jnp.broadcast_to(sent[None], square),
        jnp.broadcast_to(sent[:, None], square),
    ).reshape(n_chip, PER_CLASS, width + LANES)
    recv = lax.all_to_all(sent, "tensor", 0, 0, axis_index_groups=same_core)
    recv = recv.reshape(n_chip * PER_CLASS, width + LANES)

    vmem = pl.BlockSpec(memory_space=pltpu.VMEM)
    own = pl.pallas_call(
        pack_kernel,
        in_specs=[pl.BlockSpec(memory_space=pltpu.SMEM), vmem, vmem],
        out_specs=vmem,
        out_shape=jax.ShapeDtypeStruct((CAP, width), jnp.bfloat16),
        cost_estimate=pl.CostEstimate(
            flops=2 * CAP * LANES * width, bytes_accessed=2 * (CAP + LANES) * width, transcendentals=0
        ),
    )(lengths, recv, norm_gain[None, :])

    up = [own]
    down = [own]
    for _ in range(N_Y // 2 - 1):
        pair = (
            lax.ppermute(up[-1], "tensor", along(1)),
            lax.ppermute(down[-1], "tensor", along(-1)),
        )
        up.append(pair[0])
        down.append(pair[1])
    up.append(lax.ppermute(up[-1], "tensor", along(1)))

    vocab_dev = head_weight.shape[1]
    weight = pl.pallas_call(
        stack_kernel,
        in_specs=[pl.BlockSpec(memory_space=pl.ANY)] * (N_DP + 2),
        out_specs=vmem,
        out_shape=jax.ShapeDtypeStruct((vocab_dev, width), jnp.bfloat16),
        scratch_shapes=[pltpu.SemaphoreType.DMA((N_DP,))],
        cost_estimate=pl.CostEstimate(
            flops=0, bytes_accessed=4 * vocab_dev * width, transcendentals=0
        ),
    )(*[p.T for p in pieces], up[2], down[2])
    weights = [weight, lax.ppermute(weight, "tensor", other_core)]
    stats = run_head((0, -1, 1), lengths, [own, up[1], down[1]], weights, None)
    stats = run_head((-2, 2), lengths, [up[2], down[2]], weights, stats)
    stats = run_head((-3, 3, -4), lengths, [up[3], down[3], up[4]], weights, stats)

    sent = stats[:, :STATS].reshape(N_Y, STATS, n_chip, PER_CLASS)
    sent = sent.transpose(2, 1, 0, 3).reshape(n_chip, STATS * row_dev)
    back = lax.all_to_all(sent, "tensor", 0, 0, axis_index_groups=same_core)
    back = back.reshape(n_chip, STATS, row_dev)
    top, total, moment, chosen = (back[:, k] for k in range(STATS))
    top_own = jnp.max(top, axis=0)
    rescale = jnp.exp(top - top_own)
    total_own = jnp.sum(total * rescale, axis=0)
    moment_own = jnp.sum(moment * rescale, axis=0)
    chosen_own = jnp.sum(chosen, axis=0)

    own_rows = tensor_idx * row_dev + jnp.arange(row_dev, dtype=jnp.int32)
    onehot = (own_rows // SLOT)[:, None] == jnp.arange(SEQ_DP, dtype=jnp.int32)[None, :]
    length_of = jnp.sum(jnp.where(onehot, lengths[0][None, :], 0), axis=1)
    scored = own_rows % SLOT < length_of
    safe_total = jnp.where(scored, total_own, 1.0)
    lse = top_own + jnp.log(safe_total)
    logprob = jnp.where(scored, chosen_own - lse, 0.0)
    entropy = jnp.where(scored, lse - moment_own / safe_total, 0.0)
    return (logprob, entropy)


def solution(mesh):
    return jax.shard_map(
        per_device,
        mesh=mesh,
        in_specs=(
            P(("dp", "tensor"), None),
            P(),
            P("dp", "tensor"),
            P(("dp", "tensor")),
            P("dp", None),
        ),
        out_specs=(P(("dp", "tensor")), P(("dp", "tensor"))),
        check_vma=False,
    )
```

```python
import functools

import jax
import jax.numpy as jnp
from jax import lax
from jax.experimental import pallas as pl
from jax.experimental.pallas import tpu as pltpu
from jax.sharding import PartitionSpec as P

SEQ_DP = 4
SLOT = 512
N_DP = 4
N_Z, N_Y, N_CORE = 8, 8, 2
PER_CLASS = 2
CAP = 72
LANES = 128
DIGIT = 64
TILE = 200
PITCH = SLOT // (N_Y * 2)
STATS = 4


def class_layout(len_ref, place, core):
    first = core * (N_Y * PER_CLASS) + place * PER_CLASS
    starts, counts, at = [], [], 0
    for s in range(SEQ_DP):
        n = jnp.clip(lax.div(len_ref[0, s] - first + (PITCH - 1), PITCH), 0, SLOT // PITCH)
        starts.append(at)
        counts.append(n * PER_CLASS)
        at = at + n * PER_CLASS
    return starts, counts


def my_place():
    t = lax.axis_index("tensor")
    core = lax.rem(t, N_CORE)
    y = lax.rem(lax.div(t, N_CORE), N_Y)
    z = lax.div(t, N_CORE * N_Y)
    return jnp.where(core == 0, y, z), core


def pack_kernel(len_ref, recv_ref, gain_ref, out_ref):
    width = gain_ref.shape[1]
    mine, core = my_place()
    starts, counts = class_layout(len_ref, mine, core)
    shape = (LANES, LANES)
    k = lax.broadcasted_iota(jnp.int32, shape, 0)
    i = lax.broadcasted_iota(jnp.int32, shape, 1)
    pick = jnp.zeros(shape, jnp.float32)
    for s in range(SEQ_DP):
        rel = k - starts[s]
        hit = (rel >= 0) & (rel < counts[s]) & (i == rel + s * (PER_CLASS * SLOT // PITCH))
        pick = jnp.where(hit, 1.0, pick)
    pick = pick.astype(jnp.bfloat16)
    rows = jnp.dot(pick[:CAP], recv_ref[:, :width], preferred_element_type=jnp.float32)
    meansq = jnp.mean(rows * rows, axis=-1, keepdims=True)
    normed = rows * lax.rsqrt(meansq + 1e-06) * gain_ref[...]
    digits = lax.dot_general(
        recv_ref[:, width:],
        pick,
        (((0,), (1,)), ((), ())),
        preferred_element_type=jnp.float32,
    ).astype(jnp.bfloat16)
    shape = (CAP, LANES)
    place = lax.broadcasted_iota(jnp.int32, shape, 0) - (CAP - 3)
    place = jnp.where(place == lax.broadcasted_iota(jnp.int32, shape, 1), 1.0, 0.0)
    tail = jnp.dot(place.astype(jnp.bfloat16), digits, preferred_element_type=jnp.float32)
    out_ref[...] = normed.astype(jnp.bfloat16)
    out_ref[:, :LANES] = (normed[:, :LANES] + tail).astype(jnp.bfloat16)


def stack_kernel(own, before, after, far_top, far_low, up_ref, down_ref, out_ref, sem):
    del up_ref, down_ref
    me = lax.axis_index("dp")
    depth = own.shape[1]
    half = far_top.shape[0]
    copies = []
    for k, (piece, at, by) in enumerate(
        ((own, 0, 0), (before, 0, 3), (after, 0, 1), (far_top, 0, 2), (far_low, half, 2))
    ):
        src = lax.rem(me + by, N_DP)
        cols = pl.ds(pl.multiple_of(src * depth, depth), depth)
        rows = slice(at, at + piece.shape[0])
        copies.append(pltpu.make_async_copy(piece, out_ref.at[rows, cols], sem.at[k]))
    for c in copies:
        c.start()
    for c in copies:
        c.wait()


def head_kernel(offsets, jobs, carried, final, len_ref, *refs):
    n = len(offsets)
    n_w = 1 + max(w for w, _ in jobs)
    x_refs, w_refs, refs = refs[:n], refs[n : n + n_w], refs[n + n_w :]
    if carried:
        prev_ref, refs = refs[0], refs[1:]
    out_ref, acc_ref, stat_ref, x_ref, w_ref, sem = refs
    vocab_dev = w_refs[0].shape[0]
    mine, core = my_place()
    t = lax.axis_index("tensor")
    owners = (t, t + 1 - 2 * core)
    wide = 2 * LANES
    lane = lax.broadcasted_iota(jnp.int32, (1, LANES), 1)
    per_slot = PER_CLASS * SLOT // PITCH

    loads = [pltpu.make_async_copy(r, x_ref.at[j], sem.at[j]) for j, r in enumerate(x_refs)]
    tiles = {}
    for w, _ in jobs:
        for at in range(0, vocab_dev, TILE):
            if (w, at) not in tiles:
                i = len(tiles)
                rows = w_refs[w].at[at : at + TILE, :]
                tiles[w, at] = (i, pltpu.make_async_copy(rows, w_ref.at[i], sem.at[n + i]))
    order = [copy for _, copy in tiles.values()]
    for c in [order[0]] + loads:
        c.start()
    if carried:
        acc_ref[...] = prev_ref[...]
    else:
        row = lax.broadcasted_iota(jnp.int32, acc_ref.shape, 1)
        acc_ref[...] = jnp.where(row == 0, -1e30, 0.0)
    for c in [order[0]] + loads:
        c.wait()
    for c in order[1:]:
        c.start()
    ready = {0}

    for w, picks in jobs:
        x_all = jnp.concatenate([x_ref[j] for j in picks], axis=0) if len(picks) > 1 else x_ref[picks[0]]
        width_n = len(picks) * CAP
        ids = jnp.zeros((1, wide), jnp.float32)
        for p, j in enumerate(picks):
            d = x_ref[j, CAP - 8 :, :LANES].astype(jnp.float32)
            d = (d[5:6] * DIGIT + d[6:7]) * DIGIT + d[7:8]
            d = jnp.concatenate([d, jnp.zeros_like(d)], axis=1)
            ids = ids + (pltpu.roll(d, p * CAP, 1) if p else d)
        ids = ids[:, :width_n].astype(jnp.int32)
        parts = []
        for at in range(0, vocab_dev, TILE):
            i, copy = tiles[w, at]
            if i not in ready:
                copy.wait()
                ready.add(i)
            logits = lax.dot_general(
                w_ref[i],
                x_all,
                (((1,), (1,)), ((), ())),
                preferred_element_type=jnp.float32,
            )
            row = lax.broadcasted_iota(jnp.int32, logits.shape, 0)
            top = jnp.max(logits, axis=0, keepdims=True)
            expo = jnp.exp(logits - top)
            total = jnp.sum(expo, axis=0, keepdims=True)
            moment = jnp.sum(expo * logits, axis=0, keepdims=True)
            hit = row == ids - (owners[w] * vocab_dev + at)
            chosen = jnp.sum(jnp.where(hit, logits, 0.0), axis=0, keepdims=True)
            parts.append((top, total, moment, chosen))
        top = functools.reduce(jnp.maximum, [p[0] for p in parts])
        scale = [jnp.exp(p[0] - top) for p in parts]
        stat_ref[...] = jnp.zeros_like(stat_ref)
        stat_ref[0:1, :width_n] = top
        stat_ref[1:2, :width_n] = sum(p[1] * f for p, f in zip(parts, scale))
        stat_ref[2:3, :width_n] = sum(p[2] * f for p, f in zip(parts, scale))
        stat_ref[3:4, :width_n] = sum(p[3] for p in parts)
        stats = stat_ref[...]
        for p, j in enumerate(picks):
            place = lax.rem(mine + offsets[j] + N_Y, N_Y)
            starts, _ = class_layout(len_ref, place, core)
            spread = jnp.zeros((8, LANES), jnp.float32)
            for s in range(SEQ_DP):
                shift = lax.rem(s * per_slot - p * CAP - starts[s] + 2 * wide, wide)
                moved = pltpu.roll(stats, shift, 1)[:, :LANES]
                spread = jnp.where(lane // per_slot == s, moved, spread)
            old = acc_ref[pl.ds(place, 1)][0]
            top = jnp.maximum(old[0:1], spread[0:1])
            f_old, f_new = jnp.exp(old[0:1] - top), jnp.exp(spread[0:1] - top)
            new = jnp.concatenate(
                [
                    top,
                    old[1:3] * f_old + spread[1:3] * f_new,
                    old[3:4] + spread[3:4],
                    jnp.zeros((4, LANES), jnp.float32),
                ],
                axis=0,
            )
            acc_ref[pl.ds(place, 1)] = new[None]

    if final:
        rows = jnp.concatenate([acc_ref[:, k, :] for k in range(STATS)], axis=0)
        out_ref[...] = jnp.transpose(rows)
    else:
        out_ref[...] = acc_ref[...]


def run_head(offsets, jobs, lengths, shards, weights, prev, final):
    n, n_w = len(offsets), len(weights)
    vocab_dev, width = weights[0].shape
    n_tiles = len({w for w, _ in jobs}) * (vocab_dev // TILE)
    vmem = pl.BlockSpec(memory_space=pltpu.VMEM)
    anywhere = pl.BlockSpec(memory_space=pl.ANY)
    args = [lengths, *shards, *weights] + ([] if prev is None else [prev])
    columns = sum(len(picks) for _, picks in jobs) * CAP
    shape = (LANES, STATS * N_Y) if final else (N_Y, 8, LANES)
    return pl.pallas_call(
        functools.partial(head_kernel, offsets, jobs, prev is not None, final),
        in_specs=[pl.BlockSpec(memory_space=pltpu.SMEM)]
        + [anywhere] * (n + n_w)
        + [vmem] * (len(args) - 1 - n - n_w),
        out_specs=vmem,
        out_shape=jax.ShapeDtypeStruct(shape, jnp.float32),
        scratch_shapes=[
            pltpu.VMEM((N_Y, 8, LANES), jnp.float32),
            pltpu.VMEM((8, 2 * LANES), jnp.float32),
            pltpu.VMEM((n, CAP, width), jnp.bfloat16),
            pltpu.VMEM((n_tiles, TILE, width), jnp.bfloat16),
            pltpu.SemaphoreType.DMA((n + n_tiles,)),
        ],
        cost_estimate=pl.CostEstimate(
            flops=2 * columns * width * vocab_dev,
            bytes_accessed=2 * width * (n * CAP + n_w * vocab_dev),
            transcendentals=columns * vocab_dev,
        ),
    )(*args)


def per_device(hidden, norm_gain, head_weight, token_ids, lengths):
    row_dev, width = hidden.shape
    n_t = N_Z * N_Y * N_CORE
    n_chip = N_Z * N_Y
    tensor_idx = lax.axis_index("tensor")
    same_core = [[N_CORE * k + c for k in range(n_chip)] for c in range(N_CORE)]
    other_core = [(i, i ^ 1) for i in range(n_t)]

    def along(by):
        step = []
        for i in range(n_t):
            z, y, core = i // (N_Y * N_CORE), i // N_CORE % N_Y, i % N_CORE
            if core == 0:
                y = (y + by) % N_Y
            else:
                z = (z + by) % N_Z
            step.append((i, (z * N_Y + y) * N_CORE + core))
        return step

    vocab_dev = head_weight.shape[1]
    half = vocab_dev // 2
    ahead = [(i, (i + 1) % N_DP) for i in range(N_DP)]
    behind = [(i, (i - 1) % N_DP) for i in range(N_DP)]
    from_before = lax.ppermute(head_weight, "dp", ahead)
    from_after = lax.ppermute(head_weight, "dp", behind)
    pieces = [
        head_weight,
        from_before,
        from_after,
        lax.ppermute(from_before[:, :half], "dp", ahead),
        lax.ppermute(from_after[:, half:], "dp", behind),
    ]

    digits = jnp.stack(
        [token_ids // (DIGIT * DIGIT), token_ids // DIGIT % DIGIT, token_ids % DIGIT], axis=1
    ).astype(jnp.bfloat16)
    digits = jnp.pad(digits, ((0, 0), (0, LANES - 3)))
    sent = jnp.concatenate([hidden, digits], axis=1).reshape(N_Y, PER_CLASS, width + LANES)
    square = (N_Z, N_Y) + sent.shape[1:]
    sent = jnp.where(
        tensor_idx % N_CORE == 0,
        jnp.broadcast_to(sent[None], square),
        jnp.broadcast_to(sent[:, None], square),
    ).reshape(n_chip, PER_CLASS, width + LANES)
    recv = lax.all_to_all(sent, "tensor", 0, 0, axis_index_groups=same_core)
    recv = recv.reshape(n_chip * PER_CLASS, width + LANES)

    vmem = pl.BlockSpec(memory_space=pltpu.VMEM)
    own = pl.pallas_call(
        pack_kernel,
        in_specs=[pl.BlockSpec(memory_space=pltpu.SMEM), vmem, vmem],
        out_specs=vmem,
        out_shape=jax.ShapeDtypeStruct((CAP, width), jnp.bfloat16),
        cost_estimate=pl.CostEstimate(
            flops=2 * CAP * LANES * width, bytes_accessed=2 * (CAP + LANES) * width, transcendentals=0
        ),
    )(lengths, recv, norm_gain[None, :])

    up = [own]
    down = [own]
    for _ in range(N_Y // 2 - 1):
        pair = (
            lax.ppermute(up[-1], "tensor", along(1)),
            lax.ppermute(down[-1], "tensor", along(-1)),
        )
        up.append(pair[0])
        down.append(pair[1])
    up.append(lax.ppermute(up[-1], "tensor", along(1)))

    weight = pl.pallas_call(
        stack_kernel,
        in_specs=[pl.BlockSpec(memory_space=pl.ANY)] * (len(pieces) + 2),
        out_specs=vmem,
        out_shape=jax.ShapeDtypeStruct((vocab_dev, width), jnp.bfloat16),
        scratch_shapes=[pltpu.SemaphoreType.DMA((len(pieces),))],
        cost_estimate=pl.CostEstimate(
            flops=0, bytes_accessed=4 * vocab_dev * width, transcendentals=0
        ),
    )(*[p.T for p in pieces], up[3], down[3])
    weights = [weight, lax.ppermute(weight, "tensor", other_core)]
    shards = [own, up[1], down[1], up[2], down[2], up[3], down[3], up[4]]
    offsets = (0, -1, 1, -2, 2, -3, 3, -4)
    early = ((0, (0, 1, 2)), (0, (3, 4)), (0, (5, 6)))
    late = ((1, (0, 1, 2)), (1, (3, 4, 5)), (1, (6, 7)), (0, (7,)))
    stats = run_head(offsets[:7], early, lengths, shards[:7], weights[:1], None, False)
    stats = run_head(offsets, late, lengths, shards, weights, stats, True)

    sent = stats.reshape(n_chip, PER_CLASS, STATS * N_Y)
    back = lax.all_to_all(sent, "tensor", 0, 0, axis_index_groups=same_core)
    back = back.reshape(n_chip, PER_CLASS, STATS, N_Y)
    top, total, moment, chosen = (back[:, :, k] for k in range(STATS))
    top_own = jnp.max(top, axis=0)
    rescale = jnp.exp(top - top_own)
    total_own = jnp.sum(total * rescale, axis=0)
    moment_own = jnp.sum(moment * rescale, axis=0)
    chosen_own = jnp.sum(chosen, axis=0)
    top_own, total_own, moment_own, chosen_own = (
        v.T.reshape(row_dev) for v in (top_own, total_own, moment_own, chosen_own)
    )

    own_rows = tensor_idx * row_dev + jnp.arange(row_dev, dtype=jnp.int32)
    onehot = (own_rows // SLOT)[:, None] == jnp.arange(SEQ_DP, dtype=jnp.int32)[None, :]
    length_of = jnp.sum(jnp.where(onehot, lengths[0][None, :], 0), axis=1)
    scored = own_rows % SLOT < length_of
    safe_total = jnp.where(scored, total_own, 1.0)
    lse = top_own + jnp.log(safe_total)
    logprob = jnp.where(scored, chosen_own - lse, 0.0)
    entropy = jnp.where(scored, lse - moment_own / safe_total, 0.0)
    return (logprob, entropy)


def solution(mesh):
    return jax.shard_map(
        per_device,
        mesh=mesh,
        in_specs=(
            P(("dp", "tensor"), None),
            P(),
            P("dp", "tensor"),
            P(("dp", "tensor")),
            P("dp", None),
        ),
        out_specs=(P(("dp", "tensor")), P(("dp", "tensor"))),
        check_vma=False,
    )
```

```python
import functools

import jax
import jax.numpy as jnp
from jax import lax
from jax.experimental import pallas as pl
from jax.experimental.pallas import tpu as pltpu
from jax.sharding import PartitionSpec as P

SEQ_DP = 4
SLOT = 512
N_LINE = 8
N_CORE = 2
LANES = 128
DIGIT = 64
BLOCK = 16
LIVE = 34
STATS = 4
TILE = 400
PITCH = BLOCK * N_CORE
PER_SLOT = SLOT // PITCH


def block_starts(len_ref, core):
    starts, at = [], 0
    for s in range(SEQ_DP):
        starts.append(at)
        n = lax.div(len_ref[0, s] - core * BLOCK + (PITCH - 1), PITCH)
        at = at + jnp.clip(n, 0, PER_SLOT)
    return starts, at


def owner_of(k, starts):
    owner = k
    for s in range(1, SEQ_DP):
        owner = jnp.where(k >= starts[s], k - starts[s] + s * PER_SLOT, owner)
    return owner


def norm_kernel(hidden_ref, gain_ref, digit_ref, out_ref):
    wide = hidden_ref[...].astype(jnp.float32)
    meansq = jnp.mean(wide * wide, axis=-1, keepdims=True)
    normed = (wide * lax.rsqrt(meansq + 1e-06) * gain_ref[...]).astype(jnp.bfloat16)
    both = jnp.concatenate([normed, digit_ref[...]], axis=1)
    for j in range(N_LINE):
        out_ref[j] = both


def head_kernel(len_ref, h_ref, own_ref, other_ref, out_ref, x_ref, w_ref, sem):
    vocab_dev, width = own_ref.shape
    t = lax.axis_index("tensor")
    core = lax.rem(t, N_CORE)
    owners = (t, t + 1 - 2 * core)
    starts, total_blocks = block_starts(len_ref, core)

    loads = []
    for k in range(LIVE):
        owner = jnp.minimum(owner_of(k, starts), N_LINE * N_LINE - 1)
        z, y = lax.div(owner, N_LINE), lax.rem(owner, N_LINE)
        line = jnp.where(core == 0, y, z)
        row = jnp.where(core == 0, z, y) * BLOCK
        block = h_ref.at[line, pl.ds(pl.multiple_of(row, BLOCK), BLOCK), :]
        loads.append(pltpu.make_async_copy(block, x_ref.at[k], sem.at[k]))
    tiles = []
    for half, ref in enumerate((own_ref, other_ref)):
        for at in range(0, vocab_dev, TILE):
            i = len(tiles)
            copy = pltpu.make_async_copy(
                ref.at[at : at + TILE, :], w_ref.at[i], sem.at[LIVE + i]
            )
            tiles.append((copy, owners[half] * vocab_dev + at))
    tiles[0][0].start()
    for c in loads:
        c.start()
    for c in loads:
        c.wait()
    for copy, _ in tiles[1:]:
        copy.start()

    n = LIVE * BLOCK
    x_all = x_ref[:, :, :width].reshape(n, width)
    extra = x_ref[:, :, width:].reshape(n, LANES)
    eye = lax.broadcasted_iota(jnp.int32, (8, LANES), 0) == lax.broadcasted_iota(
        jnp.int32, (8, LANES), 1
    )
    d = lax.dot_general(
        jnp.where(eye, 1.0, 0.0).astype(jnp.bfloat16),
        extra,
        (((1,), (1,)), ((), ())),
        preferred_element_type=jnp.float32,
    )
    ids = ((d[0:1] * DIGIT + d[1:2]) * DIGIT + d[2:3]).astype(jnp.int32)

    parts = []
    for i, (copy, first) in enumerate(tiles):
        copy.wait()
        logits = lax.dot_general(
            w_ref[i],
            x_all,
            (((1,), (1,)), ((), ())),
            preferred_element_type=jnp.float32,
        )
        row = lax.broadcasted_iota(jnp.int32, logits.shape, 0)
        top = jnp.max(logits, axis=0, keepdims=True)
        expo = jnp.exp(logits - top)
        total = jnp.sum(expo, axis=0, keepdims=True)
        moment = jnp.sum(expo * logits, axis=0, keepdims=True)
        hit = row == ids - first
        chosen = jnp.sum(jnp.where(hit, logits, 0.0), axis=0, keepdims=True)
        parts.append((top, total, moment, chosen))
    top = functools.reduce(jnp.maximum, [p[0] for p in parts])
    scale = [jnp.exp(p[0] - top) for p in parts]
    stats = (
        top,
        sum(p[1] * f for p, f in zip(parts, scale)),
        sum(p[2] * f for p, f in zip(parts, scale)),
        sum(p[3] for p in parts),
    )

    lane = lax.broadcasted_iota(jnp.int32, (1, n), 1)
    block = lane // BLOCK
    owner = jnp.where(block < total_blocks, owner_of(block, starts), -1)
    chips = N_LINE * N_LINE
    mine = owner == lax.broadcasted_iota(jnp.int32, (chips, n), 0)
    place = lax.broadcasted_iota(jnp.int32, (n, STATS * BLOCK), 0) % BLOCK
    column = lax.broadcasted_iota(jnp.int32, (n, STATS * BLOCK), 1)
    out = jnp.zeros((chips, STATS * BLOCK), jnp.float32)
    for k, stat in enumerate(stats):
        spot = jnp.where(column == place + k * BLOCK, 1.0, 0.0)
        out = out + jnp.dot(
            jnp.where(mine, stat, 0.0),
            spot,
            precision=lax.Precision.HIGHEST,
            preferred_element_type=jnp.float32,
        )
    out_ref[...] = out


def run_head(lengths, lines, own, other):
    vocab_dev, width = own.shape
    n_tiles = 2 * vocab_dev // TILE
    anywhere = pl.BlockSpec(memory_space=pl.ANY)
    n = LIVE * BLOCK
    return pl.pallas_call(
        head_kernel,
        in_specs=[pl.BlockSpec(memory_space=pltpu.SMEM)] + [anywhere] * 3,
        out_specs=pl.BlockSpec(memory_space=pltpu.VMEM),
        out_shape=jax.ShapeDtypeStruct((N_LINE * N_LINE, STATS * BLOCK), jnp.float32),
        scratch_shapes=[
            pltpu.VMEM((LIVE, BLOCK, width + LANES), jnp.bfloat16),
            pltpu.VMEM((n_tiles, TILE, width), jnp.bfloat16),
            pltpu.SemaphoreType.DMA((LIVE + n_tiles,)),
        ],
        cost_estimate=pl.CostEstimate(
            flops=4 * n * width * vocab_dev,
            bytes_accessed=2 * width * (n + 2 * vocab_dev),
            transcendentals=2 * n * vocab_dev,
        ),
    )(lengths, lines, own, other)


def per_device(hidden, norm_gain, head_weight, token_ids, lengths):
    row_dev, width = hidden.shape
    vocab_dev = head_weight.shape[1]
    n_chip = N_LINE * N_LINE
    n_t = n_chip * N_CORE
    tensor_idx = lax.axis_index("tensor")
    same_core = [[N_CORE * k + c for k in range(n_chip)] for c in range(N_CORE)]
    other_core = [(i, i ^ 1) for i in range(n_t)]
    along_z = [[[(z * N_LINE + y) * N_CORE + c for z in range(N_LINE)] for y in range(N_LINE)] for c in range(N_CORE)]
    along_y = [[[(z * N_LINE + y) * N_CORE + c for y in range(N_LINE)] for z in range(N_LINE)] for c in range(N_CORE)]
    first_lines = along_z[0] + along_y[1]
    second_lines = along_y[0] + along_z[1]

    weight = lax.all_gather(head_weight, "dp", axis=0, tiled=True).T

    vmem = pl.BlockSpec(memory_space=pltpu.VMEM)
    digits = jnp.stack(
        [token_ids // (DIGIT * DIGIT), token_ids // DIGIT % DIGIT, token_ids % DIGIT], axis=1
    ).astype(jnp.bfloat16)
    digits = jnp.pad(digits, ((0, 0), (0, LANES - 3)))
    block = pl.pallas_call(
        norm_kernel,
        in_specs=[vmem] * 3,
        out_specs=vmem,
        out_shape=jax.ShapeDtypeStruct((N_LINE, row_dev, width + LANES), jnp.bfloat16),
    )(hidden, norm_gain[None, :], digits)
    line = lax.all_to_all(block, "tensor", 0, 0, axis_index_groups=first_lines)
    fan = jnp.broadcast_to(line[None], (N_LINE,) + line.shape)
    fan = fan.reshape(N_LINE, N_LINE * row_dev, width + LANES)
    lines = lax.all_to_all(fan, "tensor", 0, 0, axis_index_groups=second_lines)

    stats = run_head(lengths, lines, weight, lax.ppermute(weight, "tensor", other_core))

    back = lax.all_to_all(stats, "tensor", 0, 0, axis_index_groups=same_core, tiled=True)
    back = back.reshape(n_chip, STATS, row_dev)
    top, total, moment, chosen = (back[:, k] for k in range(STATS))
    top_own = jnp.max(top, axis=0)
    rescale = jnp.exp(top - top_own)
    total_own = jnp.sum(total * rescale, axis=0)
    moment_own = jnp.sum(moment * rescale, axis=0)
    chosen_own = jnp.sum(chosen, axis=0)

    own_rows = tensor_idx * row_dev + jnp.arange(row_dev, dtype=jnp.int32)
    onehot = (own_rows // SLOT)[:, None] == jnp.arange(SEQ_DP, dtype=jnp.int32)[None, :]
    length_of = jnp.sum(jnp.where(onehot, lengths[0][None, :], 0), axis=1)
    scored = own_rows % SLOT < length_of
    safe_total = jnp.where(scored, total_own, 1.0)
    lse = top_own + jnp.log(safe_total)
    logprob = jnp.where(scored, chosen_own - lse, 0.0)
    entropy = jnp.where(scored, lse - moment_own / safe_total, 0.0)
    return (logprob, entropy)


def solution(mesh):
    return jax.shard_map(
        per_device,
        mesh=mesh,
        in_specs=(
            P(("dp", "tensor"), None),
            P(),
            P("dp", "tensor"),
            P(("dp", "tensor")),
            P("dp", None),
        ),
        out_specs=(P(("dp", "tensor")), P(("dp", "tensor"))),
        check_vma=False,
    )
```

```python
import functools

import jax
import jax.numpy as jnp
from jax import lax
from jax.experimental import pallas as pl
from jax.experimental.pallas import tpu as pltpu
from jax.sharding import PartitionSpec as P

SEQ_DP = 4
SLOT = 512
N_LINE = 8
N_CORE = 2
LANES = 128
DIGIT = 64
BLOCK = 16
LIVE = 34
STATS = 4
TILE = 400
PITCH = BLOCK * N_CORE
PER_SLOT = SLOT // PITCH
OFFSETS = (0, -1, 1, -2, 2, -3, 3, -4)


def block_starts(len_ref, core):
    starts, at = [], 0
    for s in range(SEQ_DP):
        starts.append(at)
        n = lax.div(len_ref[0, s] - core * BLOCK + (PITCH - 1), PITCH)
        at = at + jnp.clip(n, 0, PER_SLOT)
    return starts, at


def owner_of(k, starts):
    owner = k
    for s in range(1, SEQ_DP):
        owner = jnp.where(k >= starts[s], k - starts[s] + s * PER_SLOT, owner)
    return owner


def norm_kernel(hidden_ref, gain_ref, digit_ref, out_ref):
    wide = hidden_ref[...].astype(jnp.float32)
    meansq = jnp.mean(wide * wide, axis=-1, keepdims=True)
    normed = (wide * lax.rsqrt(meansq + 1e-06) * gain_ref[...]).astype(jnp.bfloat16)
    both = jnp.concatenate([normed, digit_ref[...]], axis=1)
    for j in range(N_LINE):
        out_ref[j] = both


def head_kernel(len_ref, *refs):
    line_refs, (own_ref, other_ref, out_ref, x_ref, w_ref, sem) = refs[:N_LINE], refs[N_LINE:]
    vocab_dev, width = own_ref.shape
    t = lax.axis_index("tensor")
    core = lax.rem(t, N_CORE)
    owners = (t, t + 1 - 2 * core)
    starts, total_blocks = block_starts(len_ref, core)

    mine = jnp.where(core == 0, lax.rem(lax.div(t, N_CORE), N_LINE), lax.div(t, N_CORE * N_LINE))
    loads = []
    for offset, ref in zip(OFFSETS, line_refs):
        line = lax.rem(mine + offset + N_LINE, N_LINE)
        for m in range(N_LINE):
            owner = jnp.where(core == 0, m * N_LINE + line, line * N_LINE + m)
            slot, at = lax.div(owner, PER_SLOT), lax.rem(owner, PER_SLOT)
            live = at * PITCH + core * BLOCK < len_ref[0, slot]
            first = starts[0]
            for s in range(1, SEQ_DP):
                first = jnp.where(slot == s, starts[s], first)
            rows = ref.at[m * BLOCK : (m + 1) * BLOCK, :]
            loads.append((live, rows, first + at, len(loads)))

    def each_load(act):
        for live, rows, k, i in loads:

            @pl.when(live)
            def _(rows=rows, k=k, i=i):
                act(pltpu.make_async_copy(rows, x_ref.at[k], sem.at[i]))

    tiles = []
    for half, ref in enumerate((own_ref, other_ref)):
        for at in range(0, vocab_dev, TILE):
            i = len(tiles)
            copy = pltpu.make_async_copy(
                ref.at[at : at + TILE, :], w_ref.at[i], sem.at[N_LINE * N_LINE + i]
            )
            tiles.append((copy, owners[half] * vocab_dev + at))
    each_load(lambda copy: copy.start())
    tiles[0][0].start()
    each_load(lambda copy: copy.wait())
    for copy, _ in tiles[1:]:
        copy.start()

    n = LIVE * BLOCK
    x_all = x_ref[:, :, :width].reshape(n, width)
    extra = x_ref[:, :, width:].reshape(n, LANES)
    eye = lax.broadcasted_iota(jnp.int32, (8, LANES), 0) == lax.broadcasted_iota(
        jnp.int32, (8, LANES), 1
    )
    d = lax.dot_general(
        jnp.where(eye, 1.0, 0.0).astype(jnp.bfloat16),
        extra,
        (((1,), (1,)), ((), ())),
        preferred_element_type=jnp.float32,
    )
    ids = ((d[0:1] * DIGIT + d[1:2]) * DIGIT + d[2:3]).astype(jnp.int32)

    parts = []
    for i, (copy, first) in enumerate(tiles):
        copy.wait()
        logits = lax.dot_general(
            w_ref[i],
            x_all,
            (((1,), (1,)), ((), ())),
            preferred_element_type=jnp.float32,
        )
        row = lax.broadcasted_iota(jnp.int32, logits.shape, 0)
        top = jnp.max(logits, axis=0, keepdims=True)
        expo = jnp.exp(logits - top)
        total = jnp.sum(expo, axis=0, keepdims=True)
        moment = jnp.sum(expo * logits, axis=0, keepdims=True)
        hit = row == ids - first
        chosen = jnp.sum(jnp.where(hit, logits, 0.0), axis=0, keepdims=True)
        parts.append((top, total, moment, chosen))
    top = functools.reduce(jnp.maximum, [p[0] for p in parts])
    scale = [jnp.exp(p[0] - top) for p in parts]
    stats = (
        top,
        sum(p[1] * f for p, f in zip(parts, scale)),
        sum(p[2] * f for p, f in zip(parts, scale)),
        sum(p[3] for p in parts),
    )

    lane = lax.broadcasted_iota(jnp.int32, (1, n), 1)
    block = lane // BLOCK
    owner = jnp.where(block < total_blocks, owner_of(block, starts), -1)
    chips = N_LINE * N_LINE
    here = owner == lax.broadcasted_iota(jnp.int32, (chips, n), 0)
    rows = []
    for stat in stats:
        for _ in range(3):
            part = stat.astype(jnp.bfloat16).astype(jnp.float32)
            rows.append(jnp.where(here, part, 0.0).astype(jnp.bfloat16))
            stat = stat - part
    place = lax.broadcasted_iota(jnp.int32, (n, BLOCK), 0) % BLOCK
    spot = jnp.where(place == lax.broadcasted_iota(jnp.int32, (n, BLOCK), 1), 1.0, 0.0)
    moved = jnp.dot(
        jnp.concatenate(rows, axis=0),
        spot.astype(jnp.bfloat16),
        preferred_element_type=jnp.float32,
    ).reshape(STATS, 3, chips, BLOCK)
    moved = moved[:, 0] + moved[:, 1] + moved[:, 2]
    out_ref[...] = jnp.concatenate([moved[k] for k in range(STATS)], axis=1)


def run_head(lengths, lines, own, other):
    vocab_dev, width = own.shape
    n_tiles = 2 * vocab_dev // TILE
    anywhere = pl.BlockSpec(memory_space=pl.ANY)
    n = LIVE * BLOCK
    return pl.pallas_call(
        head_kernel,
        in_specs=[pl.BlockSpec(memory_space=pltpu.SMEM)] + [anywhere] * (N_LINE + 2),
        out_specs=pl.BlockSpec(memory_space=pltpu.VMEM),
        out_shape=jax.ShapeDtypeStruct((N_LINE * N_LINE, STATS * BLOCK), jnp.float32),
        scratch_shapes=[
            pltpu.VMEM((LIVE, BLOCK, width + LANES), jnp.bfloat16),
            pltpu.VMEM((n_tiles, TILE, width), jnp.bfloat16),
            pltpu.SemaphoreType.DMA((N_LINE * N_LINE + n_tiles,)),
        ],
        cost_estimate=pl.CostEstimate(
            flops=4 * n * width * vocab_dev,
            bytes_accessed=2 * width * (n + 2 * vocab_dev),
            transcendentals=2 * n * vocab_dev,
        ),
    )(lengths, *lines, own, other)


def per_device(hidden, norm_gain, head_weight, token_ids, lengths):
    row_dev, width = hidden.shape
    vocab_dev = head_weight.shape[1]
    n_chip = N_LINE * N_LINE
    n_t = n_chip * N_CORE
    tensor_idx = lax.axis_index("tensor")
    same_core = [[N_CORE * k + c for k in range(n_chip)] for c in range(N_CORE)]
    other_core = [(i, i ^ 1) for i in range(n_t)]
    along_z = [[(z * N_LINE + y) * N_CORE for z in range(N_LINE)] for y in range(N_LINE)]
    along_y = [[(z * N_LINE + y) * N_CORE + 1 for y in range(N_LINE)] for z in range(N_LINE)]

    def along(by):
        step = []
        for i in range(n_t):
            z, y, core = i // (N_LINE * N_CORE), i // N_CORE % N_LINE, i % N_CORE
            if core == 0:
                y = (y + by) % N_LINE
            else:
                z = (z + by) % N_LINE
            step.append((i, (z * N_LINE + y) * N_CORE + core))
        return step

    weight = lax.all_gather(head_weight, "dp", axis=0, tiled=True).T

    vmem = pl.BlockSpec(memory_space=pltpu.VMEM)
    digits = jnp.stack(
        [token_ids // (DIGIT * DIGIT), token_ids // DIGIT % DIGIT, token_ids % DIGIT], axis=1
    ).astype(jnp.bfloat16)
    digits = jnp.pad(digits, ((0, 0), (0, LANES - 3)))
    block = pl.pallas_call(
        norm_kernel,
        in_specs=[vmem] * 3,
        out_specs=vmem,
        out_shape=jax.ShapeDtypeStruct((N_LINE, row_dev, width + LANES), jnp.bfloat16),
    )(hidden, norm_gain[None, :], digits)
    line = lax.all_to_all(block, "tensor", 0, 0, axis_index_groups=along_z + along_y)
    own = line.reshape(N_LINE * row_dev, width + LANES)
    up, down = [own], [own]
    for _ in range(N_LINE // 2 - 1):
        up.append(lax.ppermute(up[-1], "tensor", along(1)))
        down.append(lax.ppermute(down[-1], "tensor", along(-1)))
    up.append(lax.ppermute(up[-1], "tensor", along(1)))
    lines = [own, up[1], down[1], up[2], down[2], up[3], down[3], up[4]]

    weight, _, _ = lax.optimization_barrier((weight, up[3], down[3]))
    stats = run_head(lengths, lines, weight, lax.ppermute(weight, "tensor", other_core))

    back = lax.all_to_all(stats, "tensor", 0, 0, axis_index_groups=same_core, tiled=True)
    back = back.reshape(n_chip, STATS, row_dev)
    top, total, moment, chosen = (back[:, k] for k in range(STATS))
    top_own = jnp.max(top, axis=0)
    rescale = jnp.exp(top - top_own)
    total_own = jnp.sum(total * rescale, axis=0)
    moment_own = jnp.sum(moment * rescale, axis=0)
    chosen_own = jnp.sum(chosen, axis=0)

    own_rows = tensor_idx * row_dev + jnp.arange(row_dev, dtype=jnp.int32)
    onehot = (own_rows // SLOT)[:, None] == jnp.arange(SEQ_DP, dtype=jnp.int32)[None, :]
    length_of = jnp.sum(jnp.where(onehot, lengths[0][None, :], 0), axis=1)
    scored = own_rows % SLOT < length_of
    safe_total = jnp.where(scored, total_own, 1.0)
    lse = top_own + jnp.log(safe_total)
    logprob = jnp.where(scored, chosen_own - lse, 0.0)
    entropy = jnp.where(scored, lse - moment_own / safe_total, 0.0)
    return (logprob, entropy)


def solution(mesh):
    return jax.shard_map(
        per_device,
        mesh=mesh,
        in_specs=(
            P(("dp", "tensor"), None),
            P(),
            P("dp", "tensor"),
            P(("dp", "tensor")),
            P("dp", None),
        ),
        out_specs=(P(("dp", "tensor")), P(("dp", "tensor"))),
        check_vma=False,
    )
```

```python
import functools

import jax
import jax.numpy as jnp
from jax import lax
from jax.experimental import pallas as pl
from jax.experimental.pallas import tpu as pltpu
from jax.sharding import PartitionSpec as P

SEQ_DP = 4
SLOT = 512
N_DP = 4
N_LINE = 8
N_CORE = 2
LANES = 128
DIGIT = 64
BLOCK = 16
LIVE = 34
STATS = 4
TILE = 400
PITCH = BLOCK * N_CORE
PER_SLOT = SLOT // PITCH
OFFSETS = (0, -1, 1, -2, 2, -3, 3, -4)


def block_starts(len_ref, core):
    starts, at = [], 0
    for s in range(SEQ_DP):
        starts.append(at)
        n = lax.div(len_ref[0, s] - core * BLOCK + (PITCH - 1), PITCH)
        at = at + jnp.clip(n, 0, PER_SLOT)
    return starts, at


def owner_of(k, starts):
    owner = k
    for s in range(1, SEQ_DP):
        owner = jnp.where(k >= starts[s], k - starts[s] + s * PER_SLOT, owner)
    return owner


def norm_kernel(hidden_ref, gain_ref, id_ref, out_ref):
    wide = hidden_ref[...].astype(jnp.float32)
    meansq = jnp.mean(wide * wide, axis=-1, keepdims=True)
    normed = (wide * lax.rsqrt(meansq + 1e-06) * gain_ref[...]).astype(jnp.bfloat16)
    rows = wide.shape[0]
    square = (rows, rows)
    eye = lax.broadcasted_iota(jnp.int32, square, 0) == lax.broadcasted_iota(jnp.int32, square, 1)
    ids = jnp.sum(jnp.where(eye, id_ref[...], 0), axis=1, keepdims=True)
    lane = lax.broadcasted_iota(jnp.int32, (rows, LANES), 1)
    shift = jnp.where(lane == 0, 12, jnp.where(lane == 1, 6, 0))
    digit = jnp.where(lane < 3, lax.shift_right_logical(ids, shift) & (DIGIT - 1), 0)
    both = jnp.concatenate([normed, digit.astype(jnp.float32).astype(jnp.bfloat16)], axis=1)
    for j in range(N_LINE):
        out_ref[j] = both


def stack_kernel(own, before, far, after, up_ref, down_ref, out_ref, sem):
    del up_ref, down_ref
    me = lax.axis_index("dp")
    depth = own.shape[1]
    copies = []
    for k, piece in enumerate((own, before, far, after)):
        src = lax.rem(me - k + N_DP, N_DP)
        cols = pl.ds(pl.multiple_of(src * depth, depth), depth)
        copies.append(pltpu.make_async_copy(piece, out_ref.at[:, cols], sem.at[k]))
    for c in copies:
        c.start()
    for c in copies:
        c.wait()


def my_core():
    t = lax.axis_index("tensor")
    core = lax.rem(t, N_CORE)
    y, z = lax.rem(lax.div(t, N_CORE), N_LINE), lax.div(t, N_CORE * N_LINE)
    return t, core, jnp.where(core == 0, y, z)


def block_copies(len_ref, line_refs, x_ref, sem):
    _, core, mine = my_core()
    starts, _ = block_starts(len_ref, core)
    loads = []
    for offset, ref in zip(OFFSETS, line_refs):
        line = lax.rem(mine + offset + N_LINE, N_LINE)
        for m in range(N_LINE):
            owner = jnp.where(core == 0, m * N_LINE + line, line * N_LINE + m)
            slot, at = lax.div(owner, PER_SLOT), lax.rem(owner, PER_SLOT)
            live = at * PITCH + core * BLOCK < len_ref[0, slot]
            first = starts[0]
            for s in range(1, SEQ_DP):
                first = jnp.where(slot == s, starts[s], first)
            rows = ref.at[m * BLOCK : (m + 1) * BLOCK, :]
            loads.append((live, rows, first + at, len(loads)))

    def each(act):
        for live, rows, k, i in loads:

            @pl.when(live)
            def _(rows=rows, k=k, i=i):
                act(pltpu.make_async_copy(rows, x_ref.at[k], sem.at[i]))

    return each


def weight_copies(ref, w_ref, base, sem, sem_base):
    out = []
    for i, at in enumerate(range(0, ref.shape[0], TILE)):
        rows = ref.at[at : at + TILE, :]
        out.append(pltpu.make_async_copy(rows, w_ref.at[base + i], sem.at[sem_base + base + i]))
    return out


def token_row(extra):
    shape = (8, LANES)
    eye = lax.broadcasted_iota(jnp.int32, shape, 0) == lax.broadcasted_iota(jnp.int32, shape, 1)
    d = lax.dot_general(
        jnp.where(eye, 1.0, 0.0).astype(jnp.bfloat16),
        extra,
        (((1,), (1,)), ((), ())),
        preferred_element_type=jnp.float32,
    )
    return ((d[0:1] * DIGIT + d[1:2]) * DIGIT + d[2:3]).astype(jnp.int32)


def tile_stats(weight, x, ids):
    logits = lax.dot_general(
        weight, x, (((1,), (1,)), ((), ())), preferred_element_type=jnp.float32
    )
    row = lax.broadcasted_iota(jnp.int32, logits.shape, 0)
    top = jnp.max(logits, axis=0, keepdims=True)
    expo = jnp.exp(logits - top)
    total = jnp.sum(expo, axis=0, keepdims=True)
    moment = jnp.sum(expo * logits, axis=0, keepdims=True)
    chosen = jnp.sum(jnp.where(row == ids, logits, 0.0), axis=0, keepdims=True)
    return (top, total, moment, chosen)


def merge(parts):
    top = functools.reduce(jnp.maximum, [p[0] for p in parts])
    scale = [jnp.exp(p[0] - top) for p in parts]
    return (
        top,
        sum(p[1] * f for p, f in zip(parts, scale)),
        sum(p[2] * f for p, f in zip(parts, scale)),
        sum(p[3] for p in parts),
    )


def to_owners(stats, owner):
    n = owner.shape[1]
    chips = N_LINE * N_LINE
    here = owner == lax.broadcasted_iota(jnp.int32, (chips, n), 0)
    rows = []
    for stat in stats:
        for _ in range(3):
            part = stat.astype(jnp.bfloat16).astype(jnp.float32)
            rows.append(jnp.where(here, part, 0.0).astype(jnp.bfloat16))
            stat = stat - part
    place = lax.broadcasted_iota(jnp.int32, (n, BLOCK), 0) % BLOCK
    spot = jnp.where(place == lax.broadcasted_iota(jnp.int32, (n, BLOCK), 1), 1.0, 0.0)
    moved = jnp.dot(
        jnp.concatenate(rows, axis=0),
        spot.astype(jnp.bfloat16),
        preferred_element_type=jnp.float32,
    ).reshape(STATS, 3, chips, BLOCK)
    moved = moved[:, 0] + moved[:, 1] + moved[:, 2]
    return [moved[k] for k in range(STATS)]


def early_kernel(len_ref, *refs):
    n_in = N_LINE - 1
    line_refs, (own_ref, out_ref, x_ref, w_ref, sem) = refs[:n_in], refs[n_in:]
    vocab_dev, width = own_ref.shape
    t, _, _ = my_core()
    each = block_copies(len_ref, line_refs, x_ref, sem)
    tiles = weight_copies(own_ref, w_ref, 0, sem, N_LINE * N_LINE)
    each(lambda copy: copy.start())
    tiles[0].start()
    each(lambda copy: copy.wait())
    for copy in tiles[1:]:
        copy.start()
    n = LIVE * BLOCK
    x = x_ref[:, :, :width].reshape(n, width)
    ids = token_row(x_ref[:, :, width:].reshape(n, LANES)) - t * vocab_dev
    parts = []
    for i, copy in enumerate(tiles):
        copy.wait()
        parts.append(tile_stats(w_ref[i], x, ids - i * TILE))
    out_ref[...] = jnp.zeros_like(out_ref)
    for k, stat in enumerate(merge(parts)):
        out_ref[k : k + 1, :] = stat


def late_kernel(len_ref, *refs):
    line_refs = refs[:N_LINE]
    own_ref, other_ref, early_ref, out_ref, x_ref, last_ref, w_ref, sem = refs[N_LINE:]
    vocab_dev, width = own_ref.shape
    t, core, mine = my_core()
    starts, total_blocks = block_starts(len_ref, core)
    line = lax.rem(mine + OFFSETS[-1] + N_LINE, N_LINE)
    sems = N_LINE * N_LINE
    each = block_copies(len_ref, line_refs, x_ref, sem)
    other = weight_copies(other_ref, w_ref, 0, sem, sems)
    own = weight_copies(own_ref, w_ref, len(other), sem, sems)
    last = pltpu.make_async_copy(line_refs[-1], last_ref, sem.at[sems + 2 * len(other)])
    each(lambda copy: copy.start())
    other[0].start()
    each(lambda copy: copy.wait())
    for copy in other[1:] + [last] + own:
        copy.start()

    n = LIVE * BLOCK
    x = x_ref[:, :, :width].reshape(n, width)
    ids = token_row(x_ref[:, :, width:].reshape(n, LANES)) - (t + 1 - 2 * core) * vocab_dev
    lane = lax.broadcasted_iota(jnp.int32, (1, n), 1) // BLOCK
    owner = jnp.where(lane < total_blocks, owner_of(lane, starts), -1)

    def line_of(o):
        return jnp.where(core == 0, o % N_LINE, o // N_LINE)

    missing = line_of(owner) == line
    parts = [
        tuple(
            jnp.where(missing, rest, early_ref[k : k + 1, :])
            for k, rest in enumerate((-1e30, 0.0, 0.0, 0.0))
        )
    ]
    for i, copy in enumerate(other):
        copy.wait()
        parts.append(tile_stats(w_ref[i], x, ids - i * TILE))
    most = to_owners(merge(parts), owner)

    last.wait()
    x = last_ref[:, :width]
    ids = token_row(last_ref[:, width:]) - t * vocab_dev
    parts = []
    for i, copy in enumerate(own):
        copy.wait()
        parts.append(tile_stats(w_ref[len(other) + i], x, ids - i * TILE))
    m = lax.broadcasted_iota(jnp.int32, (1, N_LINE * BLOCK), 1) // BLOCK
    rest = to_owners(merge(parts), jnp.where(core == 0, m * N_LINE + line, line * N_LINE + m))
    chips = N_LINE * N_LINE
    added = line_of(lax.broadcasted_iota(jnp.int32, (chips, BLOCK), 0)) == line
    rest[0] = jnp.where(added, rest[0], -1e30)
    out_ref[...] = jnp.concatenate(merge([most, rest]), axis=1)


def run_head(kernel, lengths, lines, weights, before, out_shape, scratch):
    vocab_dev, width = weights[0].shape
    n_tiles = len(weights) * (vocab_dev // TILE)
    anywhere = pl.BlockSpec(memory_space=pl.ANY)
    vmem = pl.BlockSpec(memory_space=pltpu.VMEM)
    n = LIVE * BLOCK
    return pl.pallas_call(
        kernel,
        in_specs=[pl.BlockSpec(memory_space=pltpu.SMEM)]
        + [anywhere] * (len(lines) + len(weights))
        + [vmem] * len(before),
        out_specs=vmem,
        out_shape=jax.ShapeDtypeStruct(out_shape, jnp.float32),
        scratch_shapes=[pltpu.VMEM((LIVE, BLOCK, width + LANES), jnp.bfloat16)]
        + scratch
        + [
            pltpu.VMEM((n_tiles, TILE, width), jnp.bfloat16),
            pltpu.SemaphoreType.DMA((N_LINE * N_LINE + n_tiles + 1,)),
        ],
        cost_estimate=pl.CostEstimate(
            flops=2 * n * width * vocab_dev,
            bytes_accessed=2 * width * (n + len(weights) * vocab_dev),
            transcendentals=n * vocab_dev,
        ),
    )(lengths, *lines, *weights, *before)


def per_device(hidden, norm_gain, head_weight, token_ids, lengths):
    row_dev, width = hidden.shape
    vocab_dev = head_weight.shape[1]
    n_chip = N_LINE * N_LINE
    n_t = n_chip * N_CORE
    tensor_idx = lax.axis_index("tensor")
    same_core = [[N_CORE * k + c for k in range(n_chip)] for c in range(N_CORE)]
    other_core = [(i, i ^ 1) for i in range(n_t)]
    along_z = [[(z * N_LINE + y) * N_CORE for z in range(N_LINE)] for y in range(N_LINE)]
    along_y = [[(z * N_LINE + y) * N_CORE + 1 for y in range(N_LINE)] for z in range(N_LINE)]

    def along(by):
        step = []
        for i in range(n_t):
            z, y, core = i // (N_LINE * N_CORE), i // N_CORE % N_LINE, i % N_CORE
            if core == 0:
                y = (y + by) % N_LINE
            else:
                z = (z + by) % N_LINE
            step.append((i, (z * N_LINE + y) * N_CORE + core))
        return step

    from_before, far, from_after = (
        lax.ppermute(head_weight, "dp", [(i, (i + k) % N_DP) for i in range(N_DP)])
        for k in (1, 2, 3)
    )

    vmem = pl.BlockSpec(memory_space=pltpu.VMEM)
    block = pl.pallas_call(
        norm_kernel,
        in_specs=[vmem] * 3,
        out_specs=vmem,
        out_shape=jax.ShapeDtypeStruct((N_LINE, row_dev, width + LANES), jnp.bfloat16),
    )(hidden, norm_gain[None, :], token_ids[None, :])
    line = lax.all_to_all(block, "tensor", 0, 0, axis_index_groups=along_z + along_y)
    own = line.reshape(N_LINE * row_dev, width + LANES)
    up, down = [own], [own]
    for k in range(N_LINE // 2 - 1):
        pair = (
            lax.ppermute(up[-1], "tensor", along(1)),
            lax.ppermute(down[-1], "tensor", along(-1)),
        )
        if k == 0:
            *pair, from_before, from_after = lax.optimization_barrier(
                (*pair, from_before, from_after)
            )
        if k == 1:
            *pair, far = lax.optimization_barrier((*pair, far))
        up.append(pair[0])
        down.append(pair[1])
    pieces = [head_weight, from_before, far, from_after]
    up.append(lax.ppermute(up[-1], "tensor", along(1)))
    lines = [own, up[1], down[1], up[2], down[2], up[3], down[3], up[4]]

    weight = pl.pallas_call(
        stack_kernel,
        in_specs=[pl.BlockSpec(memory_space=pl.ANY)] * (len(pieces) + 2),
        out_specs=vmem,
        out_shape=jax.ShapeDtypeStruct((vocab_dev, width), jnp.bfloat16),
        scratch_shapes=[pltpu.SemaphoreType.DMA((len(pieces),))],
        cost_estimate=pl.CostEstimate(
            flops=0, bytes_accessed=4 * vocab_dev * width, transcendentals=0
        ),
    )(*[p.T for p in pieces], up[3], down[3])
    other = lax.ppermute(weight, "tensor", other_core)
    early = run_head(
        early_kernel, lengths, lines[:-1], [weight], [], (8, LIVE * BLOCK), []
    )
    stats = run_head(
        late_kernel,
        lengths,
        lines,
        [weight, other],
        [early],
        (n_chip, STATS * BLOCK),
        [pltpu.VMEM((N_LINE * BLOCK, width + LANES), jnp.bfloat16)],
    )

    back = lax.all_to_all(stats, "tensor", 0, 0, axis_index_groups=same_core, tiled=True)
    back = back.reshape(n_chip, STATS, row_dev)
    top, total, moment, chosen = (back[:, k] for k in range(STATS))
    top_own = jnp.max(top, axis=0)
    rescale = jnp.exp(top - top_own)
    total_own = jnp.sum(total * rescale, axis=0)
    moment_own = jnp.sum(moment * rescale, axis=0)
    chosen_own = jnp.sum(chosen, axis=0)

    own_rows = tensor_idx * row_dev + jnp.arange(row_dev, dtype=jnp.int32)
    onehot = (own_rows // SLOT)[:, None] == jnp.arange(SEQ_DP, dtype=jnp.int32)[None, :]
    length_of = jnp.sum(jnp.where(onehot, lengths[0][None, :], 0), axis=1)
    scored = own_rows % SLOT < length_of
    safe_total = jnp.where(scored, total_own, 1.0)
    lse = top_own + jnp.log(safe_total)
    logprob = jnp.where(scored, chosen_own - lse, 0.0)
    entropy = jnp.where(scored, lse - moment_own / safe_total, 0.0)
    return (logprob, entropy)


def solution(mesh):
    return jax.shard_map(
        per_device,
        mesh=mesh,
        in_specs=(
            P(("dp", "tensor"), None),
            P(),
            P("dp", "tensor"),
            P(("dp", "tensor")),
            P("dp", None),
        ),
        out_specs=(P(("dp", "tensor")), P(("dp", "tensor"))),
        check_vma=False,
    )
```

```python
import functools

import jax
import jax.numpy as jnp
from jax import lax
from jax.experimental import pallas as pl
from jax.experimental.pallas import tpu as pltpu
from jax.sharding import PartitionSpec as P

SEQ_DP = 4
SLOT = 512
N_LINE = 8
N_CORE = 2
LANES = 128
DIGIT = 64
BLOCK = 16
LIVE = 34
STATS = 4
TILE = 400
PITCH = BLOCK * N_CORE
PER_SLOT = SLOT // PITCH
OFFSETS = (0, -1, 1, -2, 2, -3, 3, -4)


def block_starts(len_ref, core):
    starts, at = [], 0
    for s in range(SEQ_DP):
        starts.append(at)
        n = lax.div(len_ref[0, s] - core * BLOCK + (PITCH - 1), PITCH)
        at = at + jnp.clip(n, 0, PER_SLOT)
    return starts, at


def owner_of(k, starts):
    owner = k
    for s in range(1, SEQ_DP):
        owner = jnp.where(k >= starts[s], k - starts[s] + s * PER_SLOT, owner)
    return owner


def norm_kernel(hidden_ref, gain_ref, id_ref, out_ref):
    wide = hidden_ref[...].astype(jnp.float32)
    meansq = jnp.mean(wide * wide, axis=-1, keepdims=True)
    normed = (wide * lax.rsqrt(meansq + 1e-06) * gain_ref[...]).astype(jnp.bfloat16)
    rows = wide.shape[0]
    square = (rows, rows)
    eye = lax.broadcasted_iota(jnp.int32, square, 0) == lax.broadcasted_iota(jnp.int32, square, 1)
    ids = jnp.sum(jnp.where(eye, id_ref[...], 0), axis=1, keepdims=True)
    lane = lax.broadcasted_iota(jnp.int32, (rows, LANES), 1)
    shift = jnp.where(lane == 0, 12, jnp.where(lane == 1, 6, 0))
    digit = jnp.where(lane < 3, lax.shift_right_logical(ids, shift) & (DIGIT - 1), 0)
    both = jnp.concatenate([normed, digit.astype(jnp.float32).astype(jnp.bfloat16)], axis=1)
    for j in range(N_LINE):
        out_ref[j] = both


def my_core():
    t = lax.axis_index("tensor")
    core = lax.rem(t, N_CORE)
    y, z = lax.rem(lax.div(t, N_CORE), N_LINE), lax.div(t, N_CORE * N_LINE)
    return t, core, jnp.where(core == 0, y, z)


def block_copies(len_ref, offsets, line_refs, x_ref, sem):
    _, core, mine = my_core()
    starts, _ = block_starts(len_ref, core)
    loads = []
    for offset, ref in zip(offsets, line_refs):
        line = lax.rem(mine + offset + N_LINE, N_LINE)
        for m in range(N_LINE):
            owner = jnp.where(core == 0, m * N_LINE + line, line * N_LINE + m)
            slot, at = lax.div(owner, PER_SLOT), lax.rem(owner, PER_SLOT)
            live = at * PITCH + core * BLOCK < len_ref[0, slot]
            first = starts[0]
            for s in range(1, SEQ_DP):
                first = jnp.where(slot == s, starts[s], first)
            rows = ref.at[m * BLOCK : (m + 1) * BLOCK, :]
            loads.append((live, rows, first + at, len(loads)))

    def each(act):
        for live, rows, k, i in loads:

            @pl.when(live)
            def _(rows=rows, k=k, i=i):
                act(pltpu.make_async_copy(rows, x_ref.at[k], sem.at[i]))

    return each


def weight_copies(ref, w_ref, base, sem, sem_base):
    out = []
    for i, at in enumerate(range(0, ref.shape[0], TILE)):
        rows = ref.at[at : at + TILE, :]
        out.append(pltpu.make_async_copy(rows, w_ref.at[base + i], sem.at[sem_base + base + i]))
    return out


def token_row(extra):
    shape = (8, LANES)
    eye = lax.broadcasted_iota(jnp.int32, shape, 0) == lax.broadcasted_iota(jnp.int32, shape, 1)
    d = lax.dot_general(
        jnp.where(eye, 1.0, 0.0).astype(jnp.bfloat16),
        extra,
        (((1,), (1,)), ((), ())),
        preferred_element_type=jnp.float32,
    )
    return ((d[0:1] * DIGIT + d[1:2]) * DIGIT + d[2:3]).astype(jnp.int32)


def tile_stats(weight, x, ids):
    logits = lax.dot_general(
        weight, x, (((1,), (1,)), ((), ())), preferred_element_type=jnp.float32
    )
    row = lax.broadcasted_iota(jnp.int32, logits.shape, 0)
    top = jnp.max(logits, axis=0, keepdims=True)
    expo = jnp.exp(logits - top)
    total = jnp.sum(expo, axis=0, keepdims=True)
    moment = jnp.sum(expo * logits, axis=0, keepdims=True)
    chosen = jnp.sum(jnp.where(row == ids, logits, 0.0), axis=0, keepdims=True)
    return (top, total, moment, chosen)


def merge(parts):
    top = functools.reduce(jnp.maximum, [p[0] for p in parts])
    scale = [jnp.exp(p[0] - top) for p in parts]
    return (
        top,
        sum(p[1] * f for p, f in zip(parts, scale)),
        sum(p[2] * f for p, f in zip(parts, scale)),
        sum(p[3] for p in parts),
    )


def to_owners(stats, owner):
    n = owner.shape[1]
    chips = N_LINE * N_LINE
    here = owner == lax.broadcasted_iota(jnp.int32, (chips, n), 0)
    rows = []
    for stat in stats:
        for _ in range(3):
            part = stat.astype(jnp.bfloat16).astype(jnp.float32)
            rows.append(jnp.where(here, part, 0.0).astype(jnp.bfloat16))
            stat = stat - part
    place = lax.broadcasted_iota(jnp.int32, (n, BLOCK), 0) % BLOCK
    spot = jnp.where(place == lax.broadcasted_iota(jnp.int32, (n, BLOCK), 1), 1.0, 0.0)
    moved = jnp.dot(
        jnp.concatenate(rows, axis=0),
        spot.astype(jnp.bfloat16),
        preferred_element_type=jnp.float32,
    ).reshape(STATS, 3, chips, BLOCK)
    moved = moved[:, 0] + moved[:, 1] + moved[:, 2]
    return [moved[k] for k in range(STATS)]


def early_kernel(len_ref, *refs):
    n_in = N_LINE - 1
    line_refs, (own_ref, out_ref, x_ref, w_ref, sem) = refs[:n_in], refs[n_in:]
    vocab_dev, width = own_ref.shape
    t, _, _ = my_core()
    each = block_copies(len_ref, OFFSETS[:-1], line_refs, x_ref, sem)
    tiles = weight_copies(own_ref, w_ref, 0, sem, N_LINE * N_LINE)
    each(lambda copy: copy.start())
    tiles[0].start()
    each(lambda copy: copy.wait())
    for copy in tiles[1:]:
        copy.start()
    n = LIVE * BLOCK
    x = x_ref[:, :, :width].reshape(n, width)
    ids = token_row(x_ref[:, :, width:].reshape(n, LANES)) - t * vocab_dev
    parts = []
    for i, copy in enumerate(tiles):
        copy.wait()
        parts.append(tile_stats(w_ref[i], x, ids - i * TILE))
    out_ref[...] = jnp.zeros_like(out_ref)
    for k, stat in enumerate(merge(parts)):
        out_ref[k : k + 1, :] = stat


def late_kernel(
    len_ref, packed_ref, line_ref, own_ref, other_ref, early_ref, out_ref,
    x_ref, last_ref, w_ref, sem,
):
    vocab_dev, width = own_ref.shape
    t, core, mine = my_core()
    starts, total_blocks = block_starts(len_ref, core)
    line = lax.rem(mine + OFFSETS[-1] + N_LINE, N_LINE)
    other = weight_copies(other_ref, w_ref, 0, sem, N_LINE)
    own = weight_copies(own_ref, w_ref, len(other), sem, N_LINE)
    spare = N_LINE + 2 * len(other)
    last = pltpu.make_async_copy(line_ref, last_ref, sem.at[spare])
    half = LIVE // 2
    packed = [
        pltpu.make_async_copy(
            packed_ref.at[k * half : (k + 1) * half],
            x_ref.at[k * half : (k + 1) * half],
            sem.at[spare + 1 + k],
        )
        for k in range(2)
    ]
    for copy in packed + [other[0], last]:
        copy.start()
    for copy in packed:
        copy.wait()
    each = block_copies(len_ref, OFFSETS[-1:], [line_ref], x_ref, sem)
    each(lambda copy: copy.start())
    each(lambda copy: copy.wait())
    for copy in other[1:] + own:
        copy.start()

    n = LIVE * BLOCK
    x = x_ref[:, :, :width].reshape(n, width)
    ids = token_row(x_ref[:, :, width:].reshape(n, LANES)) - (t + 1 - 2 * core) * vocab_dev
    lane = lax.broadcasted_iota(jnp.int32, (1, n), 1) // BLOCK
    owner = jnp.where(lane < total_blocks, owner_of(lane, starts), -1)

    def line_of(o):
        return jnp.where(core == 0, o % N_LINE, o // N_LINE)

    missing = line_of(owner) == line
    parts = [
        tuple(
            jnp.where(missing, rest, early_ref[k : k + 1, :])
            for k, rest in enumerate((-1e30, 0.0, 0.0, 0.0))
        )
    ]
    for i, copy in enumerate(other):
        copy.wait()
        parts.append(tile_stats(w_ref[i], x, ids - i * TILE))
    most = to_owners(merge(parts), owner)

    last.wait()
    x = last_ref[:, :width]
    ids = token_row(last_ref[:, width:]) - t * vocab_dev
    parts = []
    for i, copy in enumerate(own):
        copy.wait()
        parts.append(tile_stats(w_ref[len(other) + i], x, ids - i * TILE))
    m = lax.broadcasted_iota(jnp.int32, (1, N_LINE * BLOCK), 1) // BLOCK
    rest = to_owners(merge(parts), jnp.where(core == 0, m * N_LINE + line, line * N_LINE + m))
    chips = N_LINE * N_LINE
    added = line_of(lax.broadcasted_iota(jnp.int32, (chips, BLOCK), 0)) == line
    rest[0] = jnp.where(added, rest[0], -1e30)
    out_ref[...] = jnp.concatenate(merge([most, rest]), axis=1)


def run_heads(lengths, lines, weight, other):
    vocab_dev, width = weight.shape
    tiles = vocab_dev // TILE
    anywhere = pl.BlockSpec(memory_space=pl.ANY)
    vmem = pl.BlockSpec(memory_space=pltpu.VMEM)
    smem = pl.BlockSpec(memory_space=pltpu.SMEM)
    n = LIVE * BLOCK
    deep = width + LANES
    cost = pl.CostEstimate(
        flops=2 * n * width * vocab_dev,
        bytes_accessed=2 * width * (n + vocab_dev),
        transcendentals=n * vocab_dev,
    )
    early, packed = pl.pallas_call(
        early_kernel,
        in_specs=[smem] + [anywhere] * N_LINE,
        out_specs=(vmem, vmem),
        out_shape=(
            jax.ShapeDtypeStruct((8, n), jnp.float32),
            jax.ShapeDtypeStruct((LIVE, BLOCK, deep), jnp.bfloat16),
        ),
        scratch_shapes=[
            pltpu.VMEM((tiles, TILE, width), jnp.bfloat16),
            pltpu.SemaphoreType.DMA((N_LINE * N_LINE + tiles,)),
        ],
        cost_estimate=cost,
    )(lengths, *lines[:-1], weight)
    return pl.pallas_call(
        late_kernel,
        in_specs=[smem] + [anywhere] * 4 + [vmem],
        out_specs=vmem,
        out_shape=jax.ShapeDtypeStruct((N_LINE * N_LINE, STATS * BLOCK), jnp.float32),
        scratch_shapes=[
            pltpu.VMEM((LIVE, BLOCK, deep), jnp.bfloat16),
            pltpu.VMEM((N_LINE * BLOCK, deep), jnp.bfloat16),
            pltpu.VMEM((2 * tiles, TILE, width), jnp.bfloat16),
            pltpu.SemaphoreType.DMA((N_LINE + 2 * tiles + 3,)),
        ],
        cost_estimate=cost,
    )(lengths, packed, lines[-1], weight, other, early)


def per_device(hidden, norm_gain, head_weight, token_ids, lengths):
    row_dev, width = hidden.shape
    vocab_dev = head_weight.shape[1]
    n_chip = N_LINE * N_LINE
    n_t = n_chip * N_CORE
    tensor_idx = lax.axis_index("tensor")
    same_core = [[N_CORE * k + c for k in range(n_chip)] for c in range(N_CORE)]
    other_core = [(i, i ^ 1) for i in range(n_t)]
    along_z = [[(z * N_LINE + y) * N_CORE for z in range(N_LINE)] for y in range(N_LINE)]
    along_y = [[(z * N_LINE + y) * N_CORE + 1 for y in range(N_LINE)] for z in range(N_LINE)]

    def along(by):
        step = []
        for i in range(n_t):
            z, y, core = i // (N_LINE * N_CORE), i // N_CORE % N_LINE, i % N_CORE
            if core == 0:
                y = (y + by) % N_LINE
            else:
                z = (z + by) % N_LINE
            step.append((i, (z * N_LINE + y) * N_CORE + core))
        return step

    weight = lax.all_gather(head_weight, "dp", axis=0, tiled=True).T

    vmem = pl.BlockSpec(memory_space=pltpu.VMEM)
    block = pl.pallas_call(
        norm_kernel,
        in_specs=[vmem] * 3,
        out_specs=vmem,
        out_shape=jax.ShapeDtypeStruct((N_LINE, row_dev, width + LANES), jnp.bfloat16),
    )(hidden, norm_gain[None, :], token_ids[None, :])
    line = lax.all_to_all(block, "tensor", 0, 0, axis_index_groups=along_z + along_y)
    own = line.reshape(N_LINE * row_dev, width + LANES)
    up, down = [own], [own]
    for _ in range(N_LINE // 2 - 1):
        up.append(lax.ppermute(up[-1], "tensor", along(1)))
        down.append(lax.ppermute(down[-1], "tensor", along(-1)))
    up.append(lax.ppermute(up[-1], "tensor", along(1)))
    lines = [own, up[1], down[1], up[2], down[2], up[3], down[3], up[4]]

    weight, _, _ = lax.optimization_barrier((weight, up[3], down[3]))
    other = lax.ppermute(weight, "tensor", other_core)
    stats = run_heads(lengths, lines, weight, other)

    back = lax.all_to_all(stats, "tensor", 0, 0, axis_index_groups=same_core, tiled=True)
    back = back.reshape(n_chip, STATS, row_dev)
    top, total, moment, chosen = (back[:, k] for k in range(STATS))
    top_own = jnp.max(top, axis=0)
    rescale = jnp.exp(top - top_own)
    total_own = jnp.sum(total * rescale, axis=0)
    moment_own = jnp.sum(moment * rescale, axis=0)
    chosen_own = jnp.sum(chosen, axis=0)

    own_rows = tensor_idx * row_dev + jnp.arange(row_dev, dtype=jnp.int32)
    onehot = (own_rows // SLOT)[:, None] == jnp.arange(SEQ_DP, dtype=jnp.int32)[None, :]
    length_of = jnp.sum(jnp.where(onehot, lengths[0][None, :], 0), axis=1)
    scored = own_rows % SLOT < length_of
    safe_total = jnp.where(scored, total_own, 1.0)
    lse = top_own + jnp.log(safe_total)
    logprob = jnp.where(scored, chosen_own - lse, 0.0)
    entropy = jnp.where(scored, lse - moment_own / safe_total, 0.0)
    return (logprob, entropy)


def solution(mesh):
    return jax.shard_map(
        per_device,
        mesh=mesh,
        in_specs=(
            P(("dp", "tensor"), None),
            P(),
            P("dp", "tensor"),
            P(("dp", "tensor")),
            P("dp", None),
        ),
        out_specs=(P(("dp", "tensor")), P(("dp", "tensor"))),
        check_vma=False,
    )
```

```python
import functools

import jax
import jax.numpy as jnp
from jax import lax
from jax.experimental import pallas as pl
from jax.experimental.pallas import tpu as pltpu
from jax.sharding import PartitionSpec as P

SEQ_DP = 4
SLOT = 512
N_LINE = 8
N_CORE = 2
LANES = 128
DIGIT = 64
BLOCK = 16
LIVE = 34
STATS = 4
TILE = 400
PITCH = BLOCK * N_CORE
PER_SLOT = SLOT // PITCH
OFFSETS = (0, -1, 1, -2, 2, -3, 3, -4)


def block_starts(len_ref, core):
    starts, at = [], 0
    for s in range(SEQ_DP):
        starts.append(at)
        n = lax.div(len_ref[0, s] - core * BLOCK + (PITCH - 1), PITCH)
        at = at + jnp.clip(n, 0, PER_SLOT)
    return starts, at


def owner_of(k, starts):
    owner = k
    for s in range(1, SEQ_DP):
        owner = jnp.where(k >= starts[s], k - starts[s] + s * PER_SLOT, owner)
    return owner


def norm_kernel(hidden_ref, gain_ref, id_ref, out_ref):
    wide = hidden_ref[...].astype(jnp.float32)
    meansq = jnp.mean(wide * wide, axis=-1, keepdims=True)
    normed = (wide * lax.rsqrt(meansq + 1e-06) * gain_ref[...]).astype(jnp.bfloat16)
    rows = wide.shape[0]
    square = (rows, rows)
    eye = lax.broadcasted_iota(jnp.int32, square, 0) == lax.broadcasted_iota(jnp.int32, square, 1)
    ids = jnp.sum(jnp.where(eye, id_ref[...], 0), axis=1, keepdims=True)
    lane = lax.broadcasted_iota(jnp.int32, (rows, LANES), 1)
    shift = jnp.where(lane == 0, 12, jnp.where(lane == 1, 6, 0))
    digit = jnp.where(lane < 3, lax.shift_right_logical(ids, shift) & (DIGIT - 1), 0)
    both = jnp.concatenate([normed, digit.astype(jnp.float32).astype(jnp.bfloat16)], axis=1)
    for j in range(N_LINE):
        out_ref[j] = both


def my_core():
    t = lax.axis_index("tensor")
    core = lax.rem(t, N_CORE)
    y, z = lax.rem(lax.div(t, N_CORE), N_LINE), lax.div(t, N_CORE * N_LINE)
    return t, core, jnp.where(core == 0, y, z)


def block_copies(len_ref, offsets, line_refs, x_ref, sem):
    _, core, mine = my_core()
    starts, _ = block_starts(len_ref, core)
    loads = []
    for offset, ref in zip(offsets, line_refs):
        line = lax.rem(mine + offset + N_LINE, N_LINE)
        for m in range(N_LINE):
            owner = jnp.where(core == 0, m * N_LINE + line, line * N_LINE + m)
            slot, at = lax.div(owner, PER_SLOT), lax.rem(owner, PER_SLOT)
            live = at * PITCH + core * BLOCK < len_ref[0, slot]
            first = starts[0]
            for s in range(1, SEQ_DP):
                first = jnp.where(slot == s, starts[s], first)
            rows = ref.at[m * BLOCK : (m + 1) * BLOCK, :]
            loads.append((live, rows, first + at, len(loads)))

    def each(act):
        for live, rows, k, i in loads:

            @pl.when(live)
            def _(rows=rows, k=k, i=i):
                act(pltpu.make_async_copy(rows, x_ref.at[k], sem.at[i]))

    return each


def weight_copies(ref, w_ref, base, sem, sem_base):
    out = []
    for i, at in enumerate(range(0, ref.shape[0], TILE)):
        rows = ref.at[at : at + TILE, :]
        out.append(pltpu.make_async_copy(rows, w_ref.at[base + i], sem.at[sem_base + base + i]))
    return out


def token_row(extra):
    shape = (8, LANES)
    eye = lax.broadcasted_iota(jnp.int32, shape, 0) == lax.broadcasted_iota(jnp.int32, shape, 1)
    d = lax.dot_general(
        jnp.where(eye, 1.0, 0.0).astype(jnp.bfloat16),
        extra,
        (((1,), (1,)), ((), ())),
        preferred_element_type=jnp.float32,
    )
    return ((d[0:1] * DIGIT + d[1:2]) * DIGIT + d[2:3]).astype(jnp.int32)


def tile_stats(weight, x, ids):
    logits = lax.dot_general(
        weight, x, (((1,), (1,)), ((), ())), preferred_element_type=jnp.float32
    )
    row = lax.broadcasted_iota(jnp.int32, logits.shape, 0)
    top = jnp.max(logits, axis=0, keepdims=True)
    expo = jnp.exp(logits - top)
    total = jnp.sum(expo, axis=0, keepdims=True)
    moment = jnp.sum(expo * logits, axis=0, keepdims=True)
    chosen = jnp.sum(jnp.where(row == ids, logits, 0.0), axis=0, keepdims=True)
    return (top, total, moment, chosen)


def merge(parts):
    top = functools.reduce(jnp.maximum, [p[0] for p in parts])
    scale = [jnp.exp(p[0] - top) for p in parts]
    return (
        top,
        sum(p[1] * f for p, f in zip(parts, scale)),
        sum(p[2] * f for p, f in zip(parts, scale)),
        sum(p[3] for p in parts),
    )


def to_owners(stats, owner):
    n = owner.shape[1]
    chips = N_LINE * N_LINE
    here = owner == lax.broadcasted_iota(jnp.int32, (chips, n), 0)
    here = jnp.where(here, 1.0, 0.0).astype(jnp.bfloat16)
    spot = lax.broadcasted_iota(jnp.int32, (BLOCK, n), 1) & (BLOCK - 1)
    spot = spot == lax.broadcasted_iota(jnp.int32, (BLOCK, n), 0)
    rows = []
    for _ in range(3):
        for k, stat in enumerate(stats):
            part = stat.astype(jnp.bfloat16).astype(jnp.float32)
            rows.append(jnp.where(spot, part, 0.0).astype(jnp.bfloat16))
            stats = stats[:k] + (stat - part,) + stats[k + 1 :]
    moved = lax.dot_general(
        jnp.concatenate(rows, axis=0),
        here,
        (((1,), (1,)), ((), ())),
        preferred_element_type=jnp.float32,
    )
    n = STATS * BLOCK
    return jnp.transpose(moved[:n] + moved[n : 2 * n] + moved[2 * n :])


def early_kernel(len_ref, *refs):
    line_refs, (own_ref, out_ref, x_ref, w_ref, sem) = refs[:N_LINE], refs[N_LINE:]
    vocab_dev, width = own_ref.shape
    t, _, _ = my_core()
    each = block_copies(len_ref, OFFSETS, line_refs, x_ref, sem)
    tiles = weight_copies(own_ref, w_ref, 0, sem, N_LINE * N_LINE)
    each(lambda copy: copy.start())
    tiles[0].start()
    each(lambda copy: copy.wait())
    for copy in tiles[1:]:
        copy.start()
    n = LIVE * BLOCK
    x = x_ref[:, :, :width].reshape(n, width)
    ids = token_row(x_ref[:, :, width:].reshape(n, LANES)) - t * vocab_dev
    parts = []
    for i, copy in enumerate(tiles):
        copy.wait()
        parts.append(tile_stats(w_ref[i], x, ids - i * TILE))
    out_ref[...] = jnp.zeros_like(out_ref)
    for k, stat in enumerate(merge(parts)):
        out_ref[k : k + 1, :] = stat


def late_kernel(len_ref, packed_ref, other_ref, early_ref, out_ref, x_ref, w_ref, sem):
    vocab_dev, width = other_ref.shape
    t, core, _ = my_core()
    starts, total_blocks = block_starts(len_ref, core)
    tiles = weight_copies(other_ref, w_ref, 0, sem, 0)
    half = LIVE // 2
    packed = [
        pltpu.make_async_copy(
            packed_ref.at[k * half : (k + 1) * half],
            x_ref.at[k * half : (k + 1) * half],
            sem.at[len(tiles) + k],
        )
        for k in range(2)
    ]
    for copy in packed + tiles:
        copy.start()
    n = LIVE * BLOCK
    lane = lax.broadcasted_iota(jnp.int32, (1, n), 1) // BLOCK
    owner = jnp.where(lane < total_blocks, owner_of(lane, starts), -1)
    for copy in packed:
        copy.wait()
    x = x_ref[:, :, :width].reshape(n, width)
    ids = token_row(x_ref[:, :, width:].reshape(n, LANES)) - (t + 1 - 2 * core) * vocab_dev
    parts = [tuple(early_ref[k : k + 1, :] for k in range(STATS))]
    for i, copy in enumerate(tiles):
        copy.wait()
        parts.append(tile_stats(w_ref[i], x, ids - i * TILE))
    used = owner >= 0
    stats = tuple(jnp.where(used, stat, 0.0) for stat in merge(parts))
    out_ref[...] = to_owners(stats, owner)


def run_heads(lengths, lines, weight, other):
    vocab_dev, width = weight.shape
    tiles = vocab_dev // TILE
    anywhere = pl.BlockSpec(memory_space=pl.ANY)
    vmem = pl.BlockSpec(memory_space=pltpu.VMEM)
    smem = pl.BlockSpec(memory_space=pltpu.SMEM)
    n = LIVE * BLOCK
    deep = width + LANES
    cost = pl.CostEstimate(
        flops=2 * n * width * vocab_dev,
        bytes_accessed=2 * width * (n + vocab_dev),
        transcendentals=n * vocab_dev,
    )
    early, packed = pl.pallas_call(
        early_kernel,
        in_specs=[smem] + [anywhere] * (N_LINE + 1),
        out_specs=(vmem, vmem),
        out_shape=(
            jax.ShapeDtypeStruct((8, n), jnp.float32),
            jax.ShapeDtypeStruct((LIVE, BLOCK, deep), jnp.bfloat16),
        ),
        scratch_shapes=[
            pltpu.VMEM((tiles, TILE, width), jnp.bfloat16),
            pltpu.SemaphoreType.DMA((N_LINE * N_LINE + tiles,)),
        ],
        cost_estimate=cost,
    )(lengths, *lines, weight)
    return pl.pallas_call(
        late_kernel,
        in_specs=[smem] + [anywhere] * 2 + [vmem],
        out_specs=vmem,
        out_shape=jax.ShapeDtypeStruct((N_LINE * N_LINE, STATS * BLOCK), jnp.float32),
        scratch_shapes=[
            pltpu.VMEM((LIVE, BLOCK, deep), jnp.bfloat16),
            pltpu.VMEM((tiles, TILE, width), jnp.bfloat16),
            pltpu.SemaphoreType.DMA((tiles + 2,)),
        ],
        cost_estimate=cost,
    )(lengths, packed, other, early)


def per_device(hidden, norm_gain, head_weight, token_ids, lengths):
    row_dev, width = hidden.shape
    vocab_dev = head_weight.shape[1]
    n_chip = N_LINE * N_LINE
    n_t = n_chip * N_CORE
    tensor_idx = lax.axis_index("tensor")
    same_core = [[N_CORE * k + c for k in range(n_chip)] for c in range(N_CORE)]
    other_core = [(i, i ^ 1) for i in range(n_t)]
    along_z = [[(z * N_LINE + y) * N_CORE for z in range(N_LINE)] for y in range(N_LINE)]
    along_y = [[(z * N_LINE + y) * N_CORE + 1 for y in range(N_LINE)] for z in range(N_LINE)]

    def along(by):
        step = []
        for i in range(n_t):
            z, y, core = i // (N_LINE * N_CORE), i // N_CORE % N_LINE, i % N_CORE
            if core == 0:
                y = (y + by) % N_LINE
            else:
                z = (z + by) % N_LINE
            step.append((i, (z * N_LINE + y) * N_CORE + core))
        return step

    weight = lax.all_gather(head_weight, "dp", axis=0, tiled=True).T

    vmem = pl.BlockSpec(memory_space=pltpu.VMEM)
    block = pl.pallas_call(
        norm_kernel,
        in_specs=[vmem] * 3,
        out_specs=vmem,
        out_shape=jax.ShapeDtypeStruct((N_LINE, row_dev, width + LANES), jnp.bfloat16),
    )(hidden, norm_gain[None, :], token_ids[None, :])
    line = lax.all_to_all(block, "tensor", 0, 0, axis_index_groups=along_z + along_y)
    own = line.reshape(N_LINE * row_dev, width + LANES)
    up, down = [own], [own]
    far = lax.ppermute(own, "tensor", along(N_LINE // 2))
    for k in range(N_LINE // 2 - 1):
        pair = (
            lax.ppermute(up[-1], "tensor", along(1)),
            lax.ppermute(down[-1], "tensor", along(-1)),
        )
        if k == 1:
            *pair, far = lax.optimization_barrier((*pair, far))
        up.append(pair[0])
        down.append(pair[1])
    lines = [own, up[1], down[1], up[2], down[2], up[3], down[3], far]

    weight, _, _ = lax.optimization_barrier((weight, up[3], down[3]))
    other = lax.ppermute(weight, "tensor", other_core)
    stats = run_heads(lengths, lines, weight, other)

    back = lax.all_to_all(stats, "tensor", 0, 0, axis_index_groups=same_core, tiled=True)
    back = back.reshape(n_chip, STATS, row_dev)
    top, total, moment, chosen = (back[:, k] for k in range(STATS))
    top_own = jnp.max(top, axis=0)
    rescale = jnp.exp(top - top_own)
    total_own = jnp.sum(total * rescale, axis=0)
    moment_own = jnp.sum(moment * rescale, axis=0)
    chosen_own = jnp.sum(chosen, axis=0)

    own_rows = tensor_idx * row_dev + jnp.arange(row_dev, dtype=jnp.int32)
    onehot = (own_rows // SLOT)[:, None] == jnp.arange(SEQ_DP, dtype=jnp.int32)[None, :]
    length_of = jnp.sum(jnp.where(onehot, lengths[0][None, :], 0), axis=1)
    scored = own_rows % SLOT < length_of
    safe_total = jnp.where(scored, total_own, 1.0)
    lse = top_own + jnp.log(safe_total)
    logprob = jnp.where(scored, chosen_own - lse, 0.0)
    entropy = jnp.where(scored, lse - moment_own / safe_total, 0.0)
    return (logprob, entropy)


def solution(mesh):
    return jax.shard_map(
        per_device,
        mesh=mesh,
        in_specs=(
            P(("dp", "tensor"), None),
            P(),
            P("dp", "tensor"),
            P(("dp", "tensor")),
            P("dp", None),
        ),
        out_specs=(P(("dp", "tensor")), P(("dp", "tensor"))),
        check_vma=False,
    )
```

```python
import functools

import jax
import jax.numpy as jnp
from jax import lax
from jax.experimental import pallas as pl
from jax.experimental.pallas import tpu as pltpu
from jax.sharding import PartitionSpec as P

SEQ_DP = 4
SLOT = 512
N_LINE = 8
N_CORE = 2
LANES = 128
DIGIT = 64
BLOCK = 16
LIVE = 34
STATS = 4
TILE = 400
PITCH = BLOCK * N_CORE
PER_SLOT = SLOT // PITCH
OFFSETS = (0, -1, 1, -2, 2, -3, 3, -4)


def block_starts(len_ref, core):
    starts, at = [], 0
    for s in range(SEQ_DP):
        starts.append(at)
        n = lax.div(len_ref[0, s] - core * BLOCK + (PITCH - 1), PITCH)
        at = at + jnp.clip(n, 0, PER_SLOT)
    return starts, at


def owner_of(k, starts):
    owner = k
    for s in range(1, SEQ_DP):
        owner = jnp.where(k >= starts[s], k - starts[s] + s * PER_SLOT, owner)
    return owner


def norm_kernel(hidden_ref, gain_ref, id_ref, out_ref):
    wide = hidden_ref[...].astype(jnp.float32)
    meansq = jnp.mean(wide * wide, axis=-1, keepdims=True)
    normed = (wide * lax.rsqrt(meansq + 1e-06) * gain_ref[...]).astype(jnp.bfloat16)
    rows = wide.shape[0]
    square = (rows, rows)
    eye = lax.broadcasted_iota(jnp.int32, square, 0) == lax.broadcasted_iota(jnp.int32, square, 1)
    ids = jnp.sum(jnp.where(eye, id_ref[...], 0), axis=1, keepdims=True)
    lane = lax.broadcasted_iota(jnp.int32, (rows, LANES), 1)
    shift = jnp.where(lane == 0, 12, jnp.where(lane == 1, 6, 0))
    digit = jnp.where(lane < 3, lax.shift_right_logical(ids, shift) & (DIGIT - 1), 0)
    both = jnp.concatenate([normed, digit.astype(jnp.float32).astype(jnp.bfloat16)], axis=1)
    for j in range(N_LINE):
        out_ref[j] = both


def my_core():
    t = lax.axis_index("tensor")
    core = lax.rem(t, N_CORE)
    y, z = lax.rem(lax.div(t, N_CORE), N_LINE), lax.div(t, N_CORE * N_LINE)
    return t, core, jnp.where(core == 0, y, z)


def block_copies(len_ref, offsets, line_refs, x_ref, sem):
    _, core, mine = my_core()
    starts, _ = block_starts(len_ref, core)
    loads = []
    for offset, ref in zip(offsets, line_refs):
        line = lax.rem(mine + offset + N_LINE, N_LINE)
        for m in range(N_LINE):
            owner = jnp.where(core == 0, m * N_LINE + line, line * N_LINE + m)
            slot, at = lax.div(owner, PER_SLOT), lax.rem(owner, PER_SLOT)
            live = at * PITCH + core * BLOCK < len_ref[0, slot]
            first = starts[0]
            for s in range(1, SEQ_DP):
                first = jnp.where(slot == s, starts[s], first)
            rows = ref.at[m * BLOCK : (m + 1) * BLOCK, :]
            loads.append((live, rows, first + at, len(loads)))

    def each(act):
        for live, rows, k, i in loads:

            @pl.when(live)
            def _(rows=rows, k=k, i=i):
                act(pltpu.make_async_copy(rows, x_ref.at[k], sem.at[i]))

    return each


def weight_copies(ref, w_ref, base, sem, sem_base):
    out = []
    for i, at in enumerate(range(0, ref.shape[0], TILE)):
        rows = ref.at[at : at + TILE, :]
        out.append(pltpu.make_async_copy(rows, w_ref.at[base + i], sem.at[sem_base + base + i]))
    return out


def token_row(extra):
    shape = (8, LANES)
    eye = lax.broadcasted_iota(jnp.int32, shape, 0) == lax.broadcasted_iota(jnp.int32, shape, 1)
    d = lax.dot_general(
        jnp.where(eye, 1.0, 0.0).astype(jnp.bfloat16),
        extra,
        (((1,), (1,)), ((), ())),
        preferred_element_type=jnp.float32,
    )
    return ((d[0:1] * DIGIT + d[1:2]) * DIGIT + d[2:3]).astype(jnp.int32)


def tile_stats(weight, x, ids):
    logits = lax.dot_general(
        weight, x, (((1,), (1,)), ((), ())), preferred_element_type=jnp.float32
    )
    row = lax.broadcasted_iota(jnp.int32, logits.shape, 0)
    top = jnp.max(logits, axis=0, keepdims=True)
    expo = jnp.exp(logits - top)
    total = jnp.sum(expo, axis=0, keepdims=True)
    moment = jnp.sum(expo * logits, axis=0, keepdims=True)
    chosen = jnp.sum(jnp.where(row == ids, logits, 0.0), axis=0, keepdims=True)
    return (top, total, moment, chosen)


def merge(parts):
    top = functools.reduce(jnp.maximum, [p[0] for p in parts])
    scale = [jnp.exp(p[0] - top) for p in parts]
    return (
        top,
        sum(p[1] * f for p, f in zip(parts, scale)),
        sum(p[2] * f for p, f in zip(parts, scale)),
        sum(p[3] for p in parts),
    )


def to_owners(stats, owner):
    n = owner.shape[1]
    chips = N_LINE * N_LINE
    here = owner == lax.broadcasted_iota(jnp.int32, (chips, n), 0)
    here = jnp.where(here, 1.0, 0.0).astype(jnp.bfloat16)
    spot = lax.broadcasted_iota(jnp.int32, (BLOCK, n), 1) & (BLOCK - 1)
    spot = spot == lax.broadcasted_iota(jnp.int32, (BLOCK, n), 0)
    rows = []
    for _ in range(3):
        for k, stat in enumerate(stats):
            part = stat.astype(jnp.bfloat16).astype(jnp.float32)
            rows.append(jnp.where(spot, part, 0.0).astype(jnp.bfloat16))
            stats = stats[:k] + (stat - part,) + stats[k + 1 :]
    moved = lax.dot_general(
        jnp.concatenate(rows, axis=0),
        here,
        (((1,), (1,)), ((), ())),
        preferred_element_type=jnp.float32,
    )
    n = STATS * BLOCK
    return jnp.transpose(moved[:n] + moved[n : 2 * n] + moved[2 * n :])


def early_kernel(len_ref, *refs):
    line_refs, (own_ref, out_ref, x_ref, w_ref, sem) = refs[:N_LINE], refs[N_LINE:]
    vocab_dev, width = own_ref.shape
    t, _, _ = my_core()
    each = block_copies(len_ref, OFFSETS, line_refs, x_ref, sem)
    tiles = weight_copies(own_ref, w_ref, 0, sem, N_LINE * N_LINE)
    each(lambda copy: copy.start())
    tiles[0].start()
    each(lambda copy: copy.wait())
    for copy in tiles[1:]:
        copy.start()
    n = LIVE * BLOCK
    x = x_ref[:, :, :width].reshape(n, width)
    ids = token_row(x_ref[:, :, width:].reshape(n, LANES)) - t * vocab_dev
    parts = []
    for i, copy in enumerate(tiles):
        copy.wait()
        parts.append(tile_stats(w_ref[i], x, ids - i * TILE))
    out_ref[...] = jnp.zeros_like(out_ref)
    for k, stat in enumerate(merge(parts)):
        out_ref[k : k + 1, :] = stat


def late_kernel(len_ref, packed_ref, other_ref, early_ref, out_ref, x_ref, w_ref, sem):
    vocab_dev, width = other_ref.shape
    t, core, _ = my_core()
    starts, total_blocks = block_starts(len_ref, core)
    tiles = weight_copies(other_ref, w_ref, 0, sem, 0)
    half = LIVE // 2
    packed = [
        pltpu.make_async_copy(
            packed_ref.at[k * half : (k + 1) * half],
            x_ref.at[k * half : (k + 1) * half],
            sem.at[len(tiles) + k],
        )
        for k in range(2)
    ]
    for copy in packed + tiles:
        copy.start()
    n = LIVE * BLOCK
    lane = lax.broadcasted_iota(jnp.int32, (1, n), 1) // BLOCK
    owner = jnp.where(lane < total_blocks, owner_of(lane, starts), -1)
    for copy in packed:
        copy.wait()
    x = x_ref[:, :, :width].reshape(n, width)
    ids = token_row(x_ref[:, :, width:].reshape(n, LANES)) - (t + 1 - 2 * core) * vocab_dev
    parts = [tuple(early_ref[k : k + 1, :] for k in range(STATS))]
    for i, copy in enumerate(tiles):
        copy.wait()
        parts.append(tile_stats(w_ref[i], x, ids - i * TILE))
    used = owner >= 0
    stats = tuple(jnp.where(used, stat, 0.0) for stat in merge(parts))
    out_ref[...] = to_owners(stats, owner)


def run_heads(lengths, lines, weight, other):
    vocab_dev, width = weight.shape
    tiles = vocab_dev // TILE
    anywhere = pl.BlockSpec(memory_space=pl.ANY)
    vmem = pl.BlockSpec(memory_space=pltpu.VMEM)
    smem = pl.BlockSpec(memory_space=pltpu.SMEM)
    n = LIVE * BLOCK
    deep = width + LANES
    cost = pl.CostEstimate(
        flops=2 * n * width * vocab_dev,
        bytes_accessed=2 * width * (n + vocab_dev),
        transcendentals=n * vocab_dev,
    )
    early, packed = pl.pallas_call(
        early_kernel,
        in_specs=[smem] + [anywhere] * (N_LINE + 1),
        out_specs=(vmem, vmem),
        out_shape=(
            jax.ShapeDtypeStruct((8, n), jnp.float32),
            jax.ShapeDtypeStruct((LIVE, BLOCK, deep), jnp.bfloat16),
        ),
        scratch_shapes=[
            pltpu.VMEM((tiles, TILE, width), jnp.bfloat16),
            pltpu.SemaphoreType.DMA((N_LINE * N_LINE + tiles,)),
        ],
        cost_estimate=cost,
    )(lengths, *lines, weight)
    return pl.pallas_call(
        late_kernel,
        in_specs=[smem] + [anywhere] * 2 + [vmem],
        out_specs=vmem,
        out_shape=jax.ShapeDtypeStruct((N_LINE * N_LINE, STATS * BLOCK), jnp.float32),
        scratch_shapes=[
            pltpu.VMEM((LIVE, BLOCK, deep), jnp.bfloat16),
            pltpu.VMEM((tiles, TILE, width), jnp.bfloat16),
            pltpu.SemaphoreType.DMA((tiles + 2,)),
        ],
        cost_estimate=cost,
    )(lengths, packed, other, early)


def per_device(hidden, norm_gain, head_weight, token_ids, lengths):
    row_dev, width = hidden.shape
    vocab_dev = head_weight.shape[1]
    n_chip = N_LINE * N_LINE
    n_t = n_chip * N_CORE
    tensor_idx = lax.axis_index("tensor")
    same_core = [[N_CORE * k + c for k in range(n_chip)] for c in range(N_CORE)]
    other_core = [(i, i ^ 1) for i in range(n_t)]
    along_z = [[(z * N_LINE + y) * N_CORE for z in range(N_LINE)] for y in range(N_LINE)]
    along_y = [[(z * N_LINE + y) * N_CORE + 1 for y in range(N_LINE)] for z in range(N_LINE)]

    def along(by):
        step = []
        for i in range(n_t):
            z, y, core = i // (N_LINE * N_CORE), i // N_CORE % N_LINE, i % N_CORE
            if core == 0:
                y = (y + by) % N_LINE
            else:
                z = (z + by) % N_LINE
            step.append((i, (z * N_LINE + y) * N_CORE + core))
        return step

    weight = lax.all_gather(head_weight, "dp", axis=0, tiled=True).T

    vmem = pl.BlockSpec(memory_space=pltpu.VMEM)
    block = pl.pallas_call(
        norm_kernel,
        in_specs=[vmem] * 3,
        out_specs=vmem,
        out_shape=jax.ShapeDtypeStruct((N_LINE, row_dev, width + LANES), jnp.bfloat16),
    )(hidden, norm_gain[None, :], token_ids[None, :])
    line = lax.all_to_all(block, "tensor", 0, 0, axis_index_groups=along_z + along_y)
    own = line.reshape(N_LINE * row_dev, width + LANES)
    up, down = [own], [own]
    far = lax.ppermute(own, "tensor", along(N_LINE // 2))
    for k in range(N_LINE // 2 - 1):
        pair = (
            lax.ppermute(up[-1], "tensor", along(1)),
            lax.ppermute(down[-1], "tensor", along(-1)),
        )
        if k == 2:
            *pair, far = lax.optimization_barrier((*pair, far))
        up.append(pair[0])
        down.append(pair[1])
    lines = [own, up[1], down[1], up[2], down[2], up[3], down[3], far]

    weight, _, _ = lax.optimization_barrier((weight, up[3], down[3]))
    other = lax.ppermute(weight, "tensor", other_core)
    stats = run_heads(lengths, lines, weight, other)

    back = lax.all_to_all(stats, "tensor", 0, 0, axis_index_groups=same_core, tiled=True)
    back = back.reshape(n_chip, STATS, row_dev)
    top, total, moment, chosen = (back[:, k] for k in range(STATS))
    top_own = jnp.max(top, axis=0)
    rescale = jnp.exp(top - top_own)
    total_own = jnp.sum(total * rescale, axis=0)
    moment_own = jnp.sum(moment * rescale, axis=0)
    chosen_own = jnp.sum(chosen, axis=0)

    own_rows = tensor_idx * row_dev + jnp.arange(row_dev, dtype=jnp.int32)
    onehot = (own_rows // SLOT)[:, None] == jnp.arange(SEQ_DP, dtype=jnp.int32)[None, :]
    length_of = jnp.sum(jnp.where(onehot, lengths[0][None, :], 0), axis=1)
    scored = own_rows % SLOT < length_of
    safe_total = jnp.where(scored, total_own, 1.0)
    lse = top_own + jnp.log(safe_total)
    logprob = jnp.where(scored, chosen_own - lse, 0.0)
    entropy = jnp.where(scored, lse - moment_own / safe_total, 0.0)
    return (logprob, entropy)


def solution(mesh):
    return jax.shard_map(
        per_device,
        mesh=mesh,
        in_specs=(
            P(("dp", "tensor"), None),
            P(),
            P("dp", "tensor"),
            P(("dp", "tensor")),
            P("dp", None),
        ),
        out_specs=(P(("dp", "tensor")), P(("dp", "tensor"))),
        check_vma=False,
    )
```

```python
import functools

import jax
import jax.numpy as jnp
from jax import lax
from jax.experimental import pallas as pl
from jax.experimental.pallas import tpu as pltpu
from jax.sharding import PartitionSpec as P

SEQ_DP = 4
SLOT = 512
N_LINE = 8
N_CORE = 2
LANES = 128
DIGIT = 64
BLOCK = 16
LIVE = 34
STATS = 4
TILE = 400
PITCH = BLOCK * N_CORE
PER_SLOT = SLOT // PITCH
OFFSETS = (0, -1, 1, -2, 2, -3, 3, -4)


def block_starts(len_ref, core):
    starts, at = [], 0
    for s in range(SEQ_DP):
        starts.append(at)
        n = lax.div(len_ref[0, s] - core * BLOCK + (PITCH - 1), PITCH)
        at = at + jnp.clip(n, 0, PER_SLOT)
    return starts, at


def owner_of(k, starts):
    owner = k
    for s in range(1, SEQ_DP):
        owner = jnp.where(k >= starts[s], k - starts[s] + s * PER_SLOT, owner)
    return owner


def norm_kernel(hidden_ref, gain_ref, id_ref, out_ref):
    wide = hidden_ref[...].astype(jnp.float32)
    meansq = jnp.mean(wide * wide, axis=-1, keepdims=True)
    normed = (wide * lax.rsqrt(meansq + 1e-06) * gain_ref[...]).astype(jnp.bfloat16)
    rows = wide.shape[0]
    square = (rows, rows)
    eye = lax.broadcasted_iota(jnp.int32, square, 0) == lax.broadcasted_iota(jnp.int32, square, 1)
    ids = jnp.sum(jnp.where(eye, id_ref[...], 0), axis=1, keepdims=True)
    lane = lax.broadcasted_iota(jnp.int32, (rows, LANES), 1)
    shift = jnp.where(lane == 0, 12, jnp.where(lane == 1, 6, 0))
    digit = jnp.where(lane < 3, lax.shift_right_logical(ids, shift) & (DIGIT - 1), 0)
    both = jnp.concatenate([normed, digit.astype(jnp.float32).astype(jnp.bfloat16)], axis=1)
    for j in range(N_LINE):
        out_ref[j] = both


def my_core():
    t = lax.axis_index("tensor")
    core = lax.rem(t, N_CORE)
    y, z = lax.rem(lax.div(t, N_CORE), N_LINE), lax.div(t, N_CORE * N_LINE)
    return t, core, jnp.where(core == 0, y, z)


def block_copies(len_ref, offsets, line_refs, x_ref, sem):
    _, core, mine = my_core()
    starts, _ = block_starts(len_ref, core)
    loads = []
    for offset, ref in zip(offsets, line_refs):
        line = lax.rem(mine + offset + N_LINE, N_LINE)
        for m in range(N_LINE):
            owner = jnp.where(core == 0, m * N_LINE + line, line * N_LINE + m)
            slot, at = lax.div(owner, PER_SLOT), lax.rem(owner, PER_SLOT)
            live = at * PITCH + core * BLOCK < len_ref[0, slot]
            first = starts[0]
            for s in range(1, SEQ_DP):
                first = jnp.where(slot == s, starts[s], first)
            rows = ref.at[m * BLOCK : (m + 1) * BLOCK, :]
            loads.append((live, rows, first + at, len(loads)))

    def each(act):
        for live, rows, k, i in loads:

            @pl.when(live)
            def _(rows=rows, k=k, i=i):
                act(pltpu.make_async_copy(rows, x_ref.at[k], sem.at[i]))

    return each


def weight_copies(ref, w_ref, base, sem, sem_base):
    out = []
    for i, at in enumerate(range(0, ref.shape[0], TILE)):
        rows = ref.at[at : at + TILE, :]
        out.append(pltpu.make_async_copy(rows, w_ref.at[base + i], sem.at[sem_base + base + i]))
    return out


def token_row(extra):
    shape = (8, LANES)
    eye = lax.broadcasted_iota(jnp.int32, shape, 0) == lax.broadcasted_iota(jnp.int32, shape, 1)
    d = lax.dot_general(
        jnp.where(eye, 1.0, 0.0).astype(jnp.bfloat16),
        extra,
        (((1,), (1,)), ((), ())),
        preferred_element_type=jnp.float32,
    )
    return ((d[0:1] * DIGIT + d[1:2]) * DIGIT + d[2:3]).astype(jnp.int32)


def tile_stats(weight, x, ids):
    logits = lax.dot_general(
        weight, x, (((1,), (1,)), ((), ())), preferred_element_type=jnp.float32
    )
    row = lax.broadcasted_iota(jnp.int32, logits.shape, 0)
    top = jnp.max(logits, axis=0, keepdims=True)
    expo = jnp.exp(logits - top)
    total = jnp.sum(expo, axis=0, keepdims=True)
    moment = jnp.sum(expo * logits, axis=0, keepdims=True)
    chosen = jnp.sum(jnp.where(row == ids, logits, 0.0), axis=0, keepdims=True)
    return (top, total, moment, chosen)


def merge(parts):
    top = functools.reduce(jnp.maximum, [p[0] for p in parts])
    scale = [jnp.exp(p[0] - top) for p in parts]
    return (
        top,
        sum(p[1] * f for p, f in zip(parts, scale)),
        sum(p[2] * f for p, f in zip(parts, scale)),
        sum(p[3] for p in parts),
    )


def to_owners(stats, owner):
    n = owner.shape[1]
    chips = N_LINE * N_LINE
    here = owner == lax.broadcasted_iota(jnp.int32, (chips, n), 0)
    here = jnp.where(here, 1.0, 0.0).astype(jnp.bfloat16)
    spot = lax.broadcasted_iota(jnp.int32, (BLOCK, n), 1) & (BLOCK - 1)
    spot = spot == lax.broadcasted_iota(jnp.int32, (BLOCK, n), 0)
    stats = tuple(jnp.where(owner >= 0, stat, 0.0) for stat in stats)
    rows = []
    for _ in range(3):
        for k, stat in enumerate(stats):
            part = stat.astype(jnp.bfloat16).astype(jnp.float32)
            rows.append(jnp.where(spot, part, 0.0).astype(jnp.bfloat16))
            stats = stats[:k] + (stat - part,) + stats[k + 1 :]
    moved = lax.dot_general(
        jnp.concatenate(rows, axis=0),
        here,
        (((1,), (1,)), ((), ())),
        preferred_element_type=jnp.float32,
    )
    n = STATS * BLOCK
    moved = jnp.transpose(moved[:n] + moved[n : 2 * n] + moved[2 * n :])
    return [moved[:, k * BLOCK : (k + 1) * BLOCK] for k in range(STATS)]


def early_kernel(len_ref, *refs):
    n_in = N_LINE - 1
    line_refs, (own_ref, out_ref, x_ref, w_ref, sem) = refs[:n_in], refs[n_in:]
    vocab_dev, width = own_ref.shape
    t, _, _ = my_core()
    each = block_copies(len_ref, OFFSETS[:-1], line_refs, x_ref, sem)
    tiles = weight_copies(own_ref, w_ref, 0, sem, N_LINE * N_LINE)
    each(lambda copy: copy.start())
    tiles[0].start()
    each(lambda copy: copy.wait())
    for copy in tiles[1:]:
        copy.start()
    n = LIVE * BLOCK
    x = x_ref[:, :, :width].reshape(n, width)
    ids = token_row(x_ref[:, :, width:].reshape(n, LANES)) - t * vocab_dev
    parts = []
    for i, copy in enumerate(tiles):
        copy.wait()
        parts.append(tile_stats(w_ref[i], x, ids - i * TILE))
    out_ref[...] = jnp.zeros_like(out_ref)
    for k, stat in enumerate(merge(parts)):
        out_ref[k : k + 1, :] = stat


def late_kernel(
    len_ref, packed_ref, line_ref, own_ref, other_ref, early_ref, out_ref,
    x_ref, last_ref, w_ref, sem,
):
    vocab_dev, width = own_ref.shape
    t, core, mine = my_core()
    starts, total_blocks = block_starts(len_ref, core)
    line = lax.rem(mine + OFFSETS[-1] + N_LINE, N_LINE)
    other = weight_copies(other_ref, w_ref, 0, sem, N_LINE)
    own = weight_copies(own_ref, w_ref, len(other), sem, N_LINE)
    spare = N_LINE + 2 * len(other)
    last = pltpu.make_async_copy(line_ref, last_ref, sem.at[spare])
    half = LIVE // 2
    packed = [
        pltpu.make_async_copy(
            packed_ref.at[k * half : (k + 1) * half],
            x_ref.at[k * half : (k + 1) * half],
            sem.at[spare + 1 + k],
        )
        for k in range(2)
    ]
    for copy in packed + [other[0], last]:
        copy.start()
    for copy in packed:
        copy.wait()
    each = block_copies(len_ref, OFFSETS[-1:], [line_ref], x_ref, sem)
    each(lambda copy: copy.start())
    each(lambda copy: copy.wait())
    for copy in other[1:]:
        copy.start()

    n = LIVE * BLOCK
    x = x_ref[:, :, :width].reshape(n, width)
    ids = token_row(x_ref[:, :, width:].reshape(n, LANES)) - (t + 1 - 2 * core) * vocab_dev
    lane = lax.broadcasted_iota(jnp.int32, (1, n), 1) // BLOCK
    owner = jnp.where(lane < total_blocks, owner_of(lane, starts), -1)

    def line_of(o):
        return jnp.where(core == 0, o % N_LINE, o // N_LINE)

    missing = line_of(owner) == line
    parts = [
        tuple(
            jnp.where(missing, rest, early_ref[k : k + 1, :])
            for k, rest in enumerate((-1e30, 0.0, 0.0, 0.0))
        )
    ]
    for i, copy in enumerate(other):
        copy.wait()
        own[i].start()
        parts.append(tile_stats(w_ref[i], x, ids - i * TILE))
    most = to_owners(merge(parts), owner)

    last.wait()
    x = last_ref[:, :width]
    ids = token_row(last_ref[:, width:]) - t * vocab_dev
    parts = []
    for i, copy in enumerate(own):
        copy.wait()
        parts.append(tile_stats(w_ref[len(other) + i], x, ids - i * TILE))
    m = lax.broadcasted_iota(jnp.int32, (1, N_LINE * BLOCK), 1) // BLOCK
    rest = to_owners(merge(parts), jnp.where(core == 0, m * N_LINE + line, line * N_LINE + m))
    chips = N_LINE * N_LINE
    added = line_of(lax.broadcasted_iota(jnp.int32, (chips, BLOCK), 0)) == line
    rest[0] = jnp.where(added, rest[0], -1e30)
    out_ref[...] = jnp.concatenate(merge([most, rest]), axis=1)


def run_heads(lengths, lines, weight, other):
    vocab_dev, width = weight.shape
    tiles = vocab_dev // TILE
    anywhere = pl.BlockSpec(memory_space=pl.ANY)
    vmem = pl.BlockSpec(memory_space=pltpu.VMEM)
    smem = pl.BlockSpec(memory_space=pltpu.SMEM)
    n = LIVE * BLOCK
    deep = width + LANES
    cost = pl.CostEstimate(
        flops=2 * n * width * vocab_dev,
        bytes_accessed=2 * width * (n + vocab_dev),
        transcendentals=n * vocab_dev,
    )
    early, packed = pl.pallas_call(
        early_kernel,
        in_specs=[smem] + [anywhere] * N_LINE,
        out_specs=(vmem, vmem),
        out_shape=(
            jax.ShapeDtypeStruct((8, n), jnp.float32),
            jax.ShapeDtypeStruct((LIVE, BLOCK, deep), jnp.bfloat16),
        ),
        scratch_shapes=[
            pltpu.VMEM((tiles, TILE, width), jnp.bfloat16),
            pltpu.SemaphoreType.DMA((N_LINE * N_LINE + tiles,)),
        ],
        cost_estimate=cost,
    )(lengths, *lines[:-1], weight)
    return pl.pallas_call(
        late_kernel,
        in_specs=[smem] + [anywhere] * 4 + [vmem],
        out_specs=vmem,
        out_shape=jax.ShapeDtypeStruct((N_LINE * N_LINE, STATS * BLOCK), jnp.float32),
        scratch_shapes=[
            pltpu.VMEM((LIVE, BLOCK, deep), jnp.bfloat16),
            pltpu.VMEM((N_LINE * BLOCK, deep), jnp.bfloat16),
            pltpu.VMEM((2 * tiles, TILE, width), jnp.bfloat16),
            pltpu.SemaphoreType.DMA((N_LINE + 2 * tiles + 3,)),
        ],
        cost_estimate=cost,
    )(lengths, packed, lines[-1], weight, other, early)


def per_device(hidden, norm_gain, head_weight, token_ids, lengths):
    row_dev, width = hidden.shape
    vocab_dev = head_weight.shape[1]
    n_chip = N_LINE * N_LINE
    n_t = n_chip * N_CORE
    tensor_idx = lax.axis_index("tensor")
    same_core = [[N_CORE * k + c for k in range(n_chip)] for c in range(N_CORE)]
    other_core = [(i, i ^ 1) for i in range(n_t)]
    along_z = [[(z * N_LINE + y) * N_CORE for z in range(N_LINE)] for y in range(N_LINE)]
    along_y = [[(z * N_LINE + y) * N_CORE + 1 for y in range(N_LINE)] for z in range(N_LINE)]

    def along(by):
        step = []
        for i in range(n_t):
            z, y, core = i // (N_LINE * N_CORE), i // N_CORE % N_LINE, i % N_CORE
            if core == 0:
                y = (y + by) % N_LINE
            else:
                z = (z + by) % N_LINE
            step.append((i, (z * N_LINE + y) * N_CORE + core))
        return step

    weight = lax.all_gather(head_weight, "dp", axis=0, tiled=True).T

    vmem = pl.BlockSpec(memory_space=pltpu.VMEM)
    block = pl.pallas_call(
        norm_kernel,
        in_specs=[vmem] * 3,
        out_specs=vmem,
        out_shape=jax.ShapeDtypeStruct((N_LINE, row_dev, width + LANES), jnp.bfloat16),
    )(hidden, norm_gain[None, :], token_ids[None, :])
    line = lax.all_to_all(block, "tensor", 0, 0, axis_index_groups=along_z + along_y)
    own = line.reshape(N_LINE * row_dev, width + LANES)
    up, down = [own], [own]
    for _ in range(N_LINE // 2 - 1):
        up.append(lax.ppermute(up[-1], "tensor", along(1)))
        down.append(lax.ppermute(down[-1], "tensor", along(-1)))
    up.append(lax.ppermute(up[-1], "tensor", along(1)))
    lines = [own, up[1], down[1], up[2], down[2], up[3], down[3], up[4]]

    weight, _, _ = lax.optimization_barrier((weight, up[3], down[3]))
    other = lax.ppermute(weight, "tensor", other_core)
    stats = run_heads(lengths, lines, weight, other)

    back = lax.all_to_all(stats, "tensor", 0, 0, axis_index_groups=same_core, tiled=True)
    back = back.reshape(n_chip, STATS, row_dev)
    top, total, moment, chosen = (back[:, k] for k in range(STATS))
    top_own = jnp.max(top, axis=0)
    rescale = jnp.exp(top - top_own)
    total_own = jnp.sum(total * rescale, axis=0)
    moment_own = jnp.sum(moment * rescale, axis=0)
    chosen_own = jnp.sum(chosen, axis=0)

    own_rows = tensor_idx * row_dev + jnp.arange(row_dev, dtype=jnp.int32)
    onehot = (own_rows // SLOT)[:, None] == jnp.arange(SEQ_DP, dtype=jnp.int32)[None, :]
    length_of = jnp.sum(jnp.where(onehot, lengths[0][None, :], 0), axis=1)
    scored = own_rows % SLOT < length_of
    safe_total = jnp.where(scored, total_own, 1.0)
    lse = top_own + jnp.log(safe_total)
    logprob = jnp.where(scored, chosen_own - lse, 0.0)
    entropy = jnp.where(scored, lse - moment_own / safe_total, 0.0)
    return (logprob, entropy)


def solution(mesh):
    return jax.shard_map(
        per_device,
        mesh=mesh,
        in_specs=(
            P(("dp", "tensor"), None),
            P(),
            P("dp", "tensor"),
            P(("dp", "tensor")),
            P("dp", None),
        ),
        out_specs=(P(("dp", "tensor")), P(("dp", "tensor"))),
        check_vma=False,
    )
```
